128 devices in a mesh: req: 8 (over y, core), exp: 16 (over z, x).
Axes of the slice: x: 4, y: 4, z: 4, core: 2. Of those that a mesh axis runs over, the one named last changes fastest.
Arguments:
- hidden: bfloat16 [16384, 2048], P(('req', 'exp')), may hold values from -6 to 6
- lengths: int32 [8, 4], P('req'), may hold values from 1 to 1536, 2048 in all within a row
- attn_gain: float32 [2048], replicated, may hold values from 0.25 to 1.75
- q_gain: float32 [128], replicated, may hold values from 1 to 4.5
- key_norm_gain: float32 [128], replicated, may hold values from 0.1 to 1.9
- w_query: bfloat16 [2048, 4096], P(None, 'exp'), may hold values from -0.125 to 0.125
- key_value_weight: bfloat16 [2048, 1024], replicated, may hold values from -0.125 to 0.125
- w_out: bfloat16 [4096, 2048], P('exp'), may hold values from -0.09375 to 0.09375
- ffn_gain: float32 [2048], replicated, may hold values from 0.25 to 1.75
- w_router: bfloat16 [2048, 128], replicated, may hold values from -0.125 to 0.125
- routes: int32 [16384, 8], P(('req', 'exp')), may hold values from 0 to 127, all different within a row; in each aligned block of 128 rows (0 to 127, 128 to 255, ...) at most 16 rows name the same one
- w_gate: bfloat16 [128, 2048, 768], P(('req', 'exp')), may hold values from -0.125 to 0.125
- w_up: bfloat16 [128, 2048, 768], P(('req', 'exp')), may hold values from -0.125 to 0.125
- w_down: bfloat16 [128, 768, 2048], P(('req', 'exp')), may hold values from -0.21875 to 0.21875
- page_table: int32 [1024], P(('req', 'exp')), may hold values from 0 to 1023, as said below
Outputs:
- layer_out: bfloat16 [16384, 2048], P(('req', 'exp'))
- kv_cache: bfloat16 [1024, 16384], P(('req', 'exp'))
The draws below stay inside these ranges and needn't reach their ends.
Inputs may be any that keep to these rules, and one draw needn't show every extreme that they name: `routes`: in the rows of one device no expert is named more than 16 times. `page_table`: every page number appears exactly once. The blocks of the device with index (r, x) go to pages held by devices with exp index x, exactly (8) // 8 of them to each req index; the device with flat index i holds pages i * (8) onwards.
All inputs are finite; a program needn't handle non-finite values.
Results may differ from the reference program's by a relative error of at most 0.013.
Values may be sent and summed in bfloat16 or wider, within the bound.
A program may use at most 128 MiB of HBM per device.

```python
import math
import jax
import jax.numpy as jnp
import numpy as np
from jax import lax

MODEL_DIM = 2048
QUERY_HEAD_COUNT = 32
KEY_VALUE_HEADS = 4
HEAD_SIZE = 128
FFE = 768
TOPK = 8
TOK_DEV = 128
PAGE_TOKENS = 16
PROMPTS = 4
EXPERTS = 128
GROUPS = 8
GROUP_TOK = 2048
TOKENS = 16384
MAXLEN = 1536
CAP = 16
TOTAL_PAGES = 1024
N_EXP = 16
DEVICES = 128


def draw_q_gain(key, part):
    return jax.random.uniform(key, (HEAD_SIZE,), jnp.float32, 1.0, 3.0)


def draw_page_table(key, part):
    columns = GROUP_TOK // TOK_DEV
    blocks_here = TOK_DEV // PAGE_TOKENS
    per_peer = blocks_here // GROUPS
    first_key, second_key = jax.random.split(key)
    order_keys = jax.random.split(first_key, GROUPS * columns)
    orders = jax.vmap(lambda one_key: jax.random.permutation(one_key, blocks_here))(order_keys)
    orders = orders.reshape(GROUPS, columns, blocks_here).astype(jnp.int32)
    slot_keys = jax.random.split(second_key, GROUPS * columns)
    slot_tables = jax.vmap(lambda one_key: jax.random.permutation(one_key, blocks_here))(slot_keys)
    slot_tables = slot_tables.reshape(GROUPS, columns, blocks_here).astype(jnp.int32)
    owners = orders // per_peer
    entries = jnp.arange(GROUPS, dtype=jnp.int32)[:, None, None] * per_peer + orders % per_peer
    column_ids = jnp.broadcast_to(jnp.arange(columns, dtype=jnp.int32)[None, :, None], owners.shape)
    slots = slot_tables[owners, column_ids, entries]
    pages = (owners * columns + column_ids) * blocks_here + slots
    return pages.reshape(-1).astype(jnp.int32)


def steps_of(own_key, dims, shards, smallest, top_value):
    def one(position, blocks):
        draws = jax.random.uniform(jax.random.fold_in(jax.random.fold_in(own_key, 6), position), (blocks,), jnp.float32, smallest / len(shards), top_value / len(shards))
        return jnp.repeat(jnp.exp(draws), dims[position] // blocks).reshape((-1,) + (1,) * (len(dims) - position - 1))

    gain = one(*shards[0])
    for cut in shards[1:]:
        gain = gain * one(*cut)
    return gain


def profile(count, total, reach, slope):
    portions = [(1 << 20) // math.isqrt(grade ** slope) + 1 for grade in range(2, count + 1)]
    surplus, counts = total - reach - (count - 1), [1] * (count - 1)
    while surplus > 0:
        movable = [i for i in range(count - 1) if counts[i] < reach]
        mass, remaining = sum([portions[i] for i in movable]), surplus
        for i in movable:
            addition = min(reach - counts[i], max(1, remaining * portions[i] // mass), surplus)
            counts[i] = counts[i] + addition
            surplus = surplus - addition
    return np.array([reach] + counts)


def uneven_parts(stream_key, amount, total, most, lean):
    if amount == 2:
        one = jax.random.randint(stream_key, (), max(1, total - most), min(most, total - 1) + 1)
        return jnp.stack([one, total - one])
    tallies = jnp.asarray(profile(amount, total, most, lean), jnp.int32)
    twos = (amount - 1) // 2
    donor, taker = tallies[1:1 + 2 * twos:2], tallies[2:2 + 2 * twos:2]
    room = jnp.minimum(donor - 1, most - taker)
    shifted = jax.random.randint(jax.random.fold_in(stream_key, 1), (twos,), 0, 1 << 20) % (room + 1)
    tallies = tallies.at[1:1 + 2 * twos:2].set(donor - shifted).at[2:2 + 2 * twos:2].set(taker + shifted)
    return tallies[jax.random.permutation(jax.random.fold_in(stream_key, 2), amount)]


def routed_block(rng, own, number, rows, number_of, top, reach, skew):
    ranking = jax.random.permutation(rng, number_of)
    packed, common = shares(number_of, rows * top, reach, skew, True), shares(number_of, rows * top, reach, skew, False)
    places = jnp.arange(number_of)

    def named(sizes, offset_by):
        used = int((sizes > 0).sum())
        fixed = max(1, used // 4)
        moved = fixed + (places - fixed + offset_by * (used - fixed)) % max(1, number_of - fixed)
        return jnp.zeros((number_of,), jnp.int32).at[ranking[jnp.where(places < fixed, places, moved)]].set(jnp.asarray(sizes, jnp.int32))

    sizes = jnp.where(number % 4 == 0, named(packed, number // 4), named(common, number - number // 4 - 1))
    mixed = jax.random.permutation(jax.random.fold_in(own, 3), number_of)
    giver, sink = mixed[0:number_of // 2 * 2:2], mixed[1:number_of // 2 * 2:2]
    margin = jnp.minimum(sizes[giver] - 1, reach - sizes[sink]) // 2
    margin = jnp.where((giver == ranking[0]) | (sink == ranking[0]) | (sizes[sink] == 0), 0, jnp.maximum(margin, 0))
    moved = jax.random.randint(jax.random.fold_in(own, 4), (number_of // 2,), 0, 1 << 20) % (margin + 1)
    sizes = sizes.at[giver].add(-moved).at[sink].add(moved)
    items = jnp.searchsorted(jnp.cumsum(sizes), jnp.arange(rows * top), side="right").astype(jnp.int32)
    grid = items.reshape(top, rows).T
    grid = grid[jax.random.permutation(jax.random.fold_in(own, 1), rows)]
    offset_by = jax.random.randint(jax.random.fold_in(own, 2), (rows, 1), 0, top)
    return jnp.take_along_axis(grid, (jnp.arange(top)[None, :] + offset_by) % top, axis=1)


def shares(amount, total, most, lean, full):
    portions = [(1 << 20) // math.isqrt(standing ** lean) + 1 for standing in range(1, amount + 1)]
    largest = most if full else min(most, max(-(-total // amount), total * portions[0] // sum(portions)))
    least = 1 if total - largest >= amount - 1 else 0
    holding, rest = [largest] + [least] * (amount - 1), total - largest - least * (amount - 1)
    while rest > 0:
        free = [i for i in range(1, amount) if holding[i] < largest] or [i for i in range(1, amount) if holding[i] < most]
        mass, left = sum([portions[i] for i in free]), rest
        for i in free:
            more = min(most - holding[i], max(1, left * portions[i] // mass), rest)
            holding[i] = holding[i] + more
            rest = rest - more
    return np.array(holding)


def centred(own_key, shape, deviation, reach, pieces=(), kind=jnp.bfloat16):
    values = deviation * jax.random.normal(own_key, shape, jnp.float32)
    if pieces:
        values = values * steps_of(own_key, shape, pieces, -0.22, 0.18)
    return jnp.clip(values, -reach, reach).astype(kind)


def setup_inputs(seed: int = 0) -> dict:
    keys = jax.random.split(jax.random.key(seed), 16)
    hidden = centred(keys[0], (TOKENS, MODEL_DIM), 1.0, 6.0, ((0, 128),))
    lengths = jax.vmap(lambda own: uneven_parts(own, PROMPTS, GROUP_TOK, MAXLEN, 2))(jax.random.split(keys[1], GROUPS)).reshape((GROUPS, PROMPTS)).astype(jnp.int32)
    attn_gain = jnp.clip(1.0 + 0.15 * jax.random.normal(keys[2], (MODEL_DIM,), jnp.float32), 0.25, 1.75)
    q_gain = draw_q_gain(jax.random.fold_in(keys[15], 71), 0)
    key_norm_gain = jnp.clip(1.0 + 0.18 * jax.random.normal(keys[4], (HEAD_SIZE,), jnp.float32), 0.1, 1.9)
    w_query = centred(keys[5], (MODEL_DIM, QUERY_HEAD_COUNT * HEAD_SIZE), MODEL_DIM ** -0.5, 0.125, ((1, 16),))
    key_value_weight = centred(keys[6], (MODEL_DIM, 2 * KEY_VALUE_HEADS * HEAD_SIZE), MODEL_DIM ** -0.5, 0.125)
    w_out = centred(keys[7], (QUERY_HEAD_COUNT * HEAD_SIZE, MODEL_DIM), (QUERY_HEAD_COUNT * HEAD_SIZE) ** -0.5, 0.09375, ((0, 16),))
    ffn_gain = jnp.clip(1.0 + 0.15 * jax.random.normal(keys[8], (MODEL_DIM,), jnp.float32), 0.25, 1.75)
    w_router = centred(keys[9], (MODEL_DIM, EXPERTS), MODEL_DIM ** -0.5, 0.125)
    routes_keys = jax.random.split(jax.random.fold_in(keys[10], 1), TOKENS // TOK_DEV)
    routes_turns = jax.random.permutation(jax.random.fold_in(keys[10], 3), TOKENS // TOK_DEV)
    routes = jax.vmap(lambda own, number: routed_block(jax.random.fold_in(keys[10], 2), own, number, TOK_DEV, EXPERTS, TOPK, CAP, 2))(routes_keys, routes_turns).reshape((TOKENS, TOPK))
    w_gate = centred(keys[11], (EXPERTS, MODEL_DIM, FFE), MODEL_DIM ** -0.5, 0.125, ((0, 128),))
    w_up = centred(keys[12], (EXPERTS, MODEL_DIM, FFE), MODEL_DIM ** -0.5, 0.125, ((0, 128),))
    w_down = centred(keys[13], (EXPERTS, FFE, MODEL_DIM), FFE ** -0.5, 0.21875, ((0, 128),))
    page_table = draw_page_table(jax.random.fold_in(keys[15], 71), 0)
    return dict(hidden=hidden, lengths=lengths, attn_gain=attn_gain, q_gain=q_gain, key_norm_gain=key_norm_gain, w_query=w_query, key_value_weight=key_value_weight, w_out=w_out, ffn_gain=ffn_gain, w_router=w_router, routes=routes, w_gate=w_gate, w_up=w_up, w_down=w_down, page_table=page_table)


EPSILON = 1e-06
THETA_BASE = 1000000.0

def rms_norm(values, scale_gain):
    values = values.astype(jnp.float32)
    factor = lax.rsqrt(lax.optimization_barrier(jnp.mean(values * values, -1, keepdims=True)) + EPSILON)
    return values * factor * scale_gain

def rotate(values, positions):
    half_dim = values.shape[-1] // 2
    freqs = THETA_BASE ** (-jnp.arange(half_dim, dtype=jnp.float32) * 2.0 / values.shape[-1])
    angles = positions.astype(jnp.float32)[:, None] * freqs[None, :]
    cosine = jnp.cos(angles)[:, None, :]
    sine = jnp.sin(angles)[:, None, :]
    first_half = values[..., :half_dim]
    second_half = values[..., half_dim:]
    return jnp.concatenate([first_half * cosine - second_half * sine, second_half * cosine + first_half * sine], -1)

def head_prepare(raw, scale_gain, positions, head_dim):
    row_count = raw.shape[0]
    split_heads = raw.reshape(row_count, raw.shape[1] // head_dim, head_dim)
    return rotate(rms_norm(split_heads, scale_gain), positions).reshape(row_count, raw.shape[1]).astype(jnp.bfloat16)

def layout(prompt_lengths, row_count):
    prompt_lengths = prompt_lengths.astype(jnp.int32)
    ends = jnp.cumsum(prompt_lengths).astype(jnp.int32)
    starts = ends - prompt_lengths
    index = jnp.arange(row_count, dtype=jnp.int32)
    inside = (index[:, None] >= starts[None, :]) & (index[:, None] < ends[None, :])
    labels = jnp.arange(prompt_lengths.shape[0], dtype=jnp.int32)
    prompt = lax.optimization_barrier(jnp.sum(jnp.where(inside, labels[None, :], 0), 1)).astype(jnp.int32)
    token_position = (index - lax.optimization_barrier(jnp.sum(jnp.where(inside, starts[None, :], 0), 1))).astype(jnp.int32)
    return (prompt, token_position)

def attend(query, key_rows, values_in, prompt, token_position, head_dim):
    row_count = query.shape[0]
    head_count = query.shape[1] // head_dim
    block_rows = min(512, row_count)
    block_list = row_count // block_rows
    query_blocks = query.reshape(block_list, block_rows, head_count, head_dim)

    def one_block(args):
        query_part, prompt_part, position_part = args
        scores = jnp.einsum('qhd,kd->hqk', query_part.astype(jnp.float32), key_rows.astype(jnp.float32)) / math.sqrt(head_dim)
        allowed = (prompt_part[:, None] == prompt[None, :]) & (token_position[None, :] <= position_part[:, None])
        scores = jnp.where(allowed[None], scores, -1e+30)
        highest = lax.optimization_barrier(jnp.max(scores, -1, keepdims=True))
        weights = jnp.exp(scores - highest)
        soft = (weights / lax.optimization_barrier(jnp.sum(weights, -1, keepdims=True))).astype(jnp.bfloat16)
        mixed = jnp.einsum('hqk,kd->qhd', soft.astype(jnp.float32), values_in.astype(jnp.float32))
        return mixed.reshape(block_rows, head_count * head_dim).astype(jnp.bfloat16)
    result = lax.map(one_block, (query_blocks, prompt.reshape(block_list, block_rows), token_position.reshape(block_list, block_rows)))
    return result.reshape(row_count, head_count * head_dim)

def reference(hidden, lengths, attn_gain, q_gain, key_norm_gain, w_query, key_value_weight, w_out, ffn_gain, w_router, routes, w_gate, w_up, w_down, page_table):
    normed = rms_norm(hidden, attn_gain).astype(jnp.bfloat16)
    prompt_parts = []
    position_parts = []
    for group_index in range(GROUPS):
        prompt_one, position_one = layout(lengths[group_index], GROUP_TOK)
        prompt_parts.append(prompt_one)
        position_parts.append(position_one)
    prompt = jnp.concatenate(prompt_parts, 0)
    token_position = jnp.concatenate(position_parts, 0)
    query = head_prepare(jnp.dot(normed, w_query, preferred_element_type=jnp.float32), q_gain, token_position, HEAD_SIZE)
    key_value = jnp.dot(normed, key_value_weight, preferred_element_type=jnp.float32)
    key_rows = head_prepare(key_value[:, :KEY_VALUE_HEADS * HEAD_SIZE], key_norm_gain, token_position, HEAD_SIZE)
    value_rows_all = key_value[:, KEY_VALUE_HEADS * HEAD_SIZE:].astype(jnp.bfloat16)
    group_ratio = QUERY_HEAD_COUNT // KEY_VALUE_HEADS
    group_outs = []
    for group_index in range(GROUPS):
        low = group_index * GROUP_TOK
        high = low + GROUP_TOK
        head_outs = []
        for key_value_index in range(KEY_VALUE_HEADS):
            head_outs.append(attend(query[low:high, key_value_index * group_ratio * HEAD_SIZE:(key_value_index + 1) * group_ratio * HEAD_SIZE], key_rows[low:high, key_value_index * HEAD_SIZE:(key_value_index + 1) * HEAD_SIZE], value_rows_all[low:high, key_value_index * HEAD_SIZE:(key_value_index + 1) * HEAD_SIZE], prompt[low:high], token_position[low:high], HEAD_SIZE))
        group_outs.append(jnp.concatenate(head_outs, 1))
    mixed = jnp.concatenate(group_outs, 0)
    share = QUERY_HEAD_COUNT * HEAD_SIZE // N_EXP
    projected = jnp.zeros((TOKENS, MODEL_DIM), jnp.float32)
    for part_index in range(N_EXP):
        partial_sum = jnp.dot(mixed[:, part_index * share:(part_index + 1) * share], w_out[part_index * share:(part_index + 1) * share], preferred_element_type=jnp.float32).astype(jnp.bfloat16)
        partial_sum = lax.optimization_barrier(partial_sum)
        projected = projected + partial_sum.astype(jnp.float32)
    resid = (hidden.astype(jnp.float32) + projected).astype(jnp.bfloat16)
    moe_in = rms_norm(resid, ffn_gain).astype(jnp.bfloat16)
    logits = jnp.dot(moe_in, w_router, preferred_element_type=jnp.float32)
    probs = jax.nn.softmax(logits, -1)
    picked = jnp.take_along_axis(probs, routes, 1)
    gates = picked / lax.optimization_barrier(jnp.sum(picked, 1, keepdims=True))
    flat_routes = routes.reshape(-1)
    flat_gates = gates.reshape(-1)
    limit = CAP * DEVICES

    def expert_step(running, expert_id):
        hits = flat_routes == expert_id
        found = jnp.nonzero(hits, size=limit, fill_value=0)[0].astype(jnp.int32)
        valid = (jnp.arange(limit, dtype=jnp.int32) < jnp.sum(hits.astype(jnp.int32))).astype(jnp.float32)
        token_ids = (found // TOPK).astype(jnp.int32)
        rows = moe_in[token_ids].astype(jnp.float32)
        gate_part = jnp.dot(rows, w_gate[expert_id].astype(jnp.float32), precision=lax.Precision.HIGHEST)
        up_part = jnp.dot(rows, w_up[expert_id].astype(jnp.float32), precision=lax.Precision.HIGHEST)
        act = (jax.nn.silu(gate_part) * up_part).astype(jnp.bfloat16)
        answer = jnp.dot(act.astype(jnp.float32), w_down[expert_id].astype(jnp.float32), precision=lax.Precision.HIGHEST).astype(jnp.bfloat16)
        weighted = answer.astype(jnp.float32) * (flat_gates[found] * valid)[:, None]
        return (running.at[token_ids].add(weighted), None)
    moe_sum, _ = lax.scan(expert_step, jnp.zeros((TOKENS, MODEL_DIM), jnp.float32), jnp.arange(EXPERTS, dtype=jnp.int32))
    layer_out = (resid.astype(jnp.float32) + moe_sum).astype(jnp.bfloat16)
    key_value_rows = jnp.concatenate([key_rows, value_rows_all], 1)
    block_list = key_value_rows.reshape(TOTAL_PAGES, PAGE_TOKENS * 2 * KEY_VALUE_HEADS * HEAD_SIZE)
    kv_cache = jnp.zeros_like(block_list).at[page_table].set(block_list)
    return (layer_out, kv_cache)
```

```python
import functools
import math

import jax
import jax.numpy as jnp
from jax import lax
from jax.experimental import pallas as pl
from jax.experimental.pallas import tpu as pltpu
from jax.sharding import PartitionSpec as P

EPSILON = 1e-06
THETA_BASE = 1000000.0
MESH = pl.DeviceIdType.MESH
BF = jnp.bfloat16
F32 = jnp.float32


def rms_norm(values, scale_gain):
    values = values.astype(jnp.float32)
    factor = lax.rsqrt(jnp.mean(values * values, -1, keepdims=True) + EPSILON)
    return values * factor * scale_gain


def head_norm_rope(raw, gain, cosf, sinf):
    factor = lax.rsqrt(jnp.mean(raw * raw, -1, keepdims=True) + EPSILON)
    y = raw * factor * gain
    return y * cosf + pltpu.roll(y, 64, 1) * sinf


def attention_kernel(
    normed, hidden, wq, kvw, wo, q_gain, k_gain, ffn_gain, cosf, sinf, start,
    resid_o, moe_o, rows_o,
    tok, wqa, kvv, woa, ka, va, qs, ss, peak, acc, mixed, rs, part,
    lsem, tsend, trecv, wsend, wrecv, osend, orecv, ksend, krecv, rsend, rrecv,
):
    req = lax.axis_index("req")
    col = lax.axis_index("exp")
    z = col // 4
    x = col % 4
    core = req % 2

    def dz(d):
        return (req, lax.rem(z + d, 4) * 4 + x)

    def dx(d):
        return (req, z * 4 + lax.rem(x + d, 4))

    partner = (req + 1 - 2 * core, col)
    z1, z2, z3 = lax.rem(z + 1, 4), lax.rem(z + 2, 4), lax.rem(z + 3, 4)
    x1, x2, x3 = lax.rem(x + 1, 4), lax.rem(x + 2, 4), lax.rem(x + 3, 4)
    sent = []

    def orow(xx, off, size):
        return pl.ds(pl.multiple_of(xx * 256 + off, 64), size)

    def send(src, dst, ssem, rsem, dev):
        c = pltpu.make_async_remote_copy(
            src_ref=src, dst_ref=dst, send_sem=ssem, recv_sem=rsem,
            device_id=dev, device_id_type=MESH,
        )
        c.start()
        sent.append(c)

    def got(dst, rsem, ssem):
        pltpu.make_async_remote_copy(
            src_ref=dst, dst_ref=dst, send_sem=ssem, recv_sem=rsem,
            device_id=partner, device_id_type=MESH,
        ).wait_recv()

    local_kv = pltpu.make_async_copy(kvw, kvv, lsem.at[0])
    local_kv.start()
    local_wq = pltpu.make_async_copy(wq, wqa.at[x], lsem.at[1])
    local_wq.start()
    local_wo = pltpu.make_async_copy(wo, woa.at[orow(x, 0, 256)], lsem.at[2])
    local_wo.start()
    tok[z] = normed[...]
    va[:, 128:256] = jnp.ones((2048, 128), BF)

    barrier = pltpu.get_barrier_semaphore()
    for dev in (dz(1), dz(2), dz(3), dx(1), dx(3), partner):
        pl.semaphore_signal(barrier, inc=1, device_id=dev, device_id_type=MESH)
    pl.semaphore_wait(barrier, 6)

    send(normed, tok.at[z], tsend.at[0], trecv.at[0], dz(1))
    send(normed, tok.at[z], tsend.at[1], trecv.at[1], dz(3))
    half = core * 1024
    send(wq.at[pl.ds(half, 1024)], wqa.at[x, pl.ds(half, 1024)], wsend.at[0], wrecv.at[0], dx(1))
    send(wq.at[pl.ds(half, 1024)], wqa.at[x, pl.ds(half, 1024)], wsend.at[1], wrecv.at[1], dx(3))

    def krow(zz, xx):
        return pl.ds(pl.multiple_of((zz * 4 + xx) * 128, 128), 128)

    def send_kv(zz, j):
        rows = krow(zz, x)
        k = ka.at[rows]
        v = va.at[rows, pl.ds(0, 128)]
        send(k, k, ksend.at[j, 0], krecv.at[j, 0], dx(1))
        send(v, v, ksend.at[j, 1], krecv.at[j, 1], dx(1))
        send(k, k, ksend.at[j, 2], krecv.at[j, 2], dx(3))
        send(v, v, ksend.at[j, 3], krecv.at[j, 3], dx(3))

    def relay_kv(zz, j):
        left = krow(zz, x3)
        right = krow(zz, x1)
        k = ka.at[left]
        got(k, krecv.at[j, 0], ksend.at[j, 0])
        send(k, k, ksend.at[j, 4], krecv.at[j, 4], dx(1))
        v = va.at[right, pl.ds(0, 128)]
        got(v, krecv.at[j, 3], ksend.at[j, 3])
        send(v, v, ksend.at[j, 5], krecv.at[j, 5], dx(3))

    def finish_kv(zz, j):
        left = krow(zz, x3)
        right = krow(zz, x1)
        far = krow(zz, x2)
        got(va.at[left, pl.ds(0, 128)], krecv.at[j, 1], ksend.at[j, 1])
        got(ka.at[right], krecv.at[j, 2], ksend.at[j, 2])
        got(ka.at[far], krecv.at[j, 4], ksend.at[j, 4])
        got(va.at[far, pl.ds(0, 128)], krecv.at[j, 5], ksend.at[j, 5])

    local_kv.wait()
    own = jnp.dot(normed[...], kvv[...], preferred_element_type=F32)
    for h in range(4):
        rows_o[:, h * 128 : (h + 1) * 128] = head_norm_rope(
            own[:, h * 128 : (h + 1) * 128], k_gain[...], cosf[z], sinf[z]
        ).astype(BF)
    rows_o[:, 512:1024] = own[:, 512:1024].astype(BF)
    kcols = pl.ds(pl.multiple_of(z * 128, 128), 128)
    vcols = pl.ds(pl.multiple_of(512 + z * 128, 128), 128)
    ka[krow(z, x), :] = rows_o[:, kcols]
    va[krow(z, x), 0:128] = rows_o[:, vcols]
    send_kv(z, 0)

    def make_kv(zz):
        block = tok[zz]
        kk = jnp.dot(block, kvv[:, kcols], preferred_element_type=F32)
        vv = jnp.dot(block, kvv[:, vcols], preferred_element_type=F32)
        ka[krow(zz, x), :] = head_norm_rope(kk, k_gain[...], cosf[zz], sinf[zz]).astype(BF)
        va[krow(zz, x), 0:128] = vv.astype(BF)

    got(tok.at[z3], trecv.at[0], tsend.at[0])
    send(tok.at[z3, pl.ds(0, 64)], tok.at[z3, pl.ds(0, 64)], tsend.at[2], trecv.at[2], dz(1))
    got(tok.at[z1], trecv.at[1], tsend.at[1])
    send(tok.at[z1, pl.ds(64, 64)], tok.at[z1, pl.ds(64, 64)], tsend.at[3], trecv.at[3], dz(3))
    mine = pl.ds(half, 1024)
    got(wqa.at[x3, mine], wrecv.at[0], wsend.at[0])
    r0 = wqa.at[x3, pl.ds(half, 512)]
    send(r0, r0, wsend.at[2], wrecv.at[2], dx(1))
    got(wqa.at[x1, mine], wrecv.at[1], wsend.at[1])
    r1 = wqa.at[x1, pl.ds(half + 512, 512)]
    send(r1, r1, wsend.at[3], wrecv.at[3], dx(3))
    p0 = wqa.at[x3, mine]
    send(p0, p0, wsend.at[4], wrecv.at[4], partner)
    p1 = wqa.at[x1, mine]
    send(p1, p1, wsend.at[5], wrecv.at[5], partner)

    make_kv(z3)
    send_kv(z3, 1)
    make_kv(z1)
    send_kv(z1, 2)
    relay_kv(z, 0)
    ohalf = core * 128
    omine = pl.ds(ohalf, 128)
    send(wo.at[omine], woa.at[orow(x, ohalf, 128)], osend.at[0], orecv.at[0], dx(1))
    send(wo.at[omine], woa.at[orow(x, ohalf, 128)], osend.at[1], orecv.at[1], dx(3))
    got(tok.at[z2, pl.ds(0, 64)], trecv.at[2], tsend.at[2])
    got(tok.at[z2, pl.ds(64, 64)], trecv.at[3], tsend.at[3])
    make_kv(z2)
    send_kv(z2, 3)
    relay_kv(z3, 1)
    relay_kv(z1, 2)

    got(wqa.at[x2, pl.ds(half, 512)], wrecv.at[2], wsend.at[2])
    got(wqa.at[x2, pl.ds(half + 512, 512)], wrecv.at[3], wsend.at[3])
    p2 = wqa.at[x2, mine]
    send(p2, p2, wsend.at[6], wrecv.at[6], partner)
    local_wq.wait()

    def q_slice(xx):
        for zz in range(2):
            block = jnp.concatenate([tok[2 * zz], tok[2 * zz + 1]], 0)
            raw = jnp.dot(block, wqa[xx], preferred_element_type=F32)
            for b in range(2):
                for h in range(2):
                    y = head_norm_rope(
                        raw[b * 128 : (b + 1) * 128, h * 128 : (h + 1) * 128],
                        q_gain[...], cosf[2 * zz + b], sinf[2 * zz + b],
                    )
                    row = pl.ds(pl.multiple_of((xx * 2 + h) * 128, 128), 128)
                    qs[2 * zz + b, row, :] = y.astype(BF)

    q_slice(x)
    other = pl.ds(1024 - half, 1024)
    got(wqa.at[x3, other], wrecv.at[4], wsend.at[4])
    q_slice(x3)
    relay_kv(z2, 3)
    got(wqa.at[x1, other], wrecv.at[5], wsend.at[5])
    q_slice(x1)
    got(wqa.at[x2, other], wrecv.at[6], wsend.at[6])
    q_slice(x2)

    left_o = woa.at[orow(x3, ohalf, 128)]
    right_o = woa.at[orow(x1, ohalf, 128)]
    far_o = woa.at[orow(x2, ohalf, 128)]
    got(left_o, orecv.at[0], osend.at[0])
    o0 = woa.at[orow(x3, ohalf, 64)]
    send(o0, o0, osend.at[2], orecv.at[2], dx(1))
    got(right_o, orecv.at[1], osend.at[1])
    o1 = woa.at[orow(x1, ohalf + 64, 64)]
    send(o1, o1, osend.at[3], orecv.at[3], dx(3))
    send(left_o, left_o, osend.at[4], orecv.at[4], partner)
    send(right_o, right_o, osend.at[5], orecv.at[5], partner)
    for zz, j in ((z, 0), (z3, 1), (z1, 2), (z2, 3)):
        finish_kv(zz, j)
    last_o = pltpu.make_async_remote_copy(
        src_ref=far_o, dst_ref=far_o, send_sem=osend.at[6], recv_sem=orecv.at[6],
        device_id=partner, device_id_type=MESH,
    )

    def attend(b):
        low = start[b]
        here = (b * 4 + x) * 128 + lax.broadcasted_iota(jnp.int32, (128, 512), 0)
        peak[...] = jnp.full((1024, 128), -1e30, F32)

        def score_step(c, carry):
            keys = pl.ds(pl.multiple_of(c * 512, 512), 512)
            s = lax.dot_general(
                qs[b], ka[keys, :], (((1,), (1,)), ((), ())), preferred_element_type=F32
            )
            kid = c * 512 + lax.broadcasted_iota(jnp.int32, (128, 512), 1)
            bias = jnp.where((kid >= low) & (kid <= here), 0.0, -1e30)
            s = (s.reshape(8, 128, 512) + bias[None]).reshape(1024, 512)
            ss[:, keys] = s
            top = peak[...]
            for g in range(4):
                top = jnp.maximum(top, s[:, g * 128 : (g + 1) * 128])
            peak[...] = top
            return carry

        lax.fori_loop(0, b + 1, score_step, 0)
        peak[...] = jnp.broadcast_to(jnp.max(peak[...], -1, keepdims=True), (1024, 128))
        acc[...] = jnp.zeros((1024, 256), F32)

        def mix_step(c, carry):
            keys = pl.ds(pl.multiple_of(c * 512, 512), 512)
            p = jnp.exp2(ss[:, keys] - peak[:, 0:1]).astype(BF)
            acc[...] += jnp.dot(p, va[keys, :], preferred_element_type=F32)
            return carry

        lax.fori_loop(0, b + 1, mix_step, 0)
        for h in range(8):
            rows = slice(h * 128, (h + 1) * 128)
            mixed[:, h * 128 : (h + 1) * 128] = (acc[rows, 0:128] / acc[rows, 128:256]).astype(BF)

    def share(i, off):
        b = lax.rem(z + off, 4)
        return pltpu.make_async_remote_copy(
            src_ref=part.at[b], dst_ref=rs.at[z], send_sem=rsend.at[i], recv_sem=rrecv.at[i],
            device_id=(req, b * 4 + x), device_id_type=MESH,
        )

    def block_step(i, carry):
        off = jnp.where(i == 0, 2, jnp.where(i == 1, 1, jnp.where(i == 2, 3, 0)))
        b = lax.rem(z + off, 4)
        attend(b)

        @pl.when(i == 0)
        def _():
            got(woa.at[orow(x2, ohalf, 64)], orecv.at[2], osend.at[2])
            got(woa.at[orow(x2, ohalf + 64, 64)], orecv.at[3], osend.at[3])
            last_o.start()
            got(woa.at[orow(x3, 128 - ohalf, 128)], orecv.at[4], osend.at[4])
            got(woa.at[orow(x1, 128 - ohalf, 128)], orecv.at[5], osend.at[5])
            got(woa.at[orow(x2, 128 - ohalf, 128)], orecv.at[6], osend.at[6])
            local_wo.wait()

        for n in range(2):
            cols = slice(n * 1024, (n + 1) * 1024)
            part[b, :, cols] = jnp.dot(
                mixed[...], woa[:, cols], preferred_element_type=F32
            ).astype(BF)

        @pl.when(i < 3)
        def _():
            share(i, off).start()

        return carry

    lax.fori_loop(0, 4, block_step, 0)
    for i, off in enumerate((2, 1, 3)):
        src = lax.rem(z + 4 - off, 4)
        got(rs.at[src], rrecv.at[i], rsend.at[i])
    total = hidden[...].astype(F32) + part[z].astype(F32)
    for d in range(1, 4):
        total = total + rs[lax.rem(z + d, 4)].astype(F32)
    resid = total.astype(BF)
    resid_o[...] = resid
    rf = resid.astype(F32)
    factor = lax.rsqrt(jnp.mean(rf * rf, -1, keepdims=True) + EPSILON)
    moe_o[...] = (rf * factor * ffn_gain[...]).astype(BF)
    for c in sent:
        c.wait_send()
    last_o.wait_send()
    for i, off in enumerate((2, 1, 3)):
        share(i, off).wait_send()


def attention_phase(normed, hidden, w_query, key_value_weight, w_out, q_gain, k_gain, ffn_gain, cosf, sinf, start):
    vmem = pl.BlockSpec(memory_space=pltpu.VMEM)
    hbm = pl.BlockSpec(memory_space=pl.ANY)
    dma = pltpu.SemaphoreType.DMA
    return pl.pallas_call(
        attention_kernel,
        name="attention",
        out_shape=(
            jax.ShapeDtypeStruct((128, 2048), BF),
            jax.ShapeDtypeStruct((128, 2048), BF),
            jax.ShapeDtypeStruct((128, 1024), BF),
        ),
        in_specs=[vmem, vmem, hbm, hbm, hbm, vmem, vmem, vmem, vmem, vmem, vmem],
        out_specs=(vmem, vmem, vmem),
        scratch_shapes=[
            pltpu.VMEM((4, 128, 2048), BF),
            pltpu.VMEM((4, 2048, 256), BF),
            pltpu.VMEM((2048, 1024), BF),
            pltpu.VMEM((1024, 2048), BF),
            pltpu.VMEM((2048, 128), BF),
            pltpu.VMEM((2048, 256), BF),
            pltpu.VMEM((4, 1024, 128), BF),
            pltpu.VMEM((1024, 2048), F32),
            pltpu.VMEM((1024, 128), F32),
            pltpu.VMEM((1024, 256), F32),
            pltpu.VMEM((128, 1024), BF),
            pltpu.VMEM((4, 128, 2048), BF),
            pltpu.VMEM((4, 128, 2048), BF),
            dma((3,)), dma((4,)), dma((4,)), dma((7,)), dma((7,)), dma((7,)), dma((7,)),
            dma((4, 6)), dma((4, 6)), dma((3,)), dma((3,)),
        ],
        compiler_params=pltpu.CompilerParams(
            collective_id=0, has_side_effects=True, vmem_limit_bytes=60 * 1024 * 1024
        ),
    )(normed, hidden, w_query, key_value_weight, w_out, q_gain, k_gain, ffn_gain, cosf, sinf, start)


def on_device(
    hidden,
    lengths,
    attn_gain,
    q_gain,
    key_norm_gain,
    w_query,
    key_value_weight,
    w_out,
    ffn_gain,
    w_router,
    routes,
    w_gate,
    w_up,
    w_down,
    page_table,
):
    column = lax.axis_index("exp")
    tokens_here = hidden.shape[0]
    model_width = hidden.shape[1]
    normed = rms_norm(hidden, attn_gain).astype(jnp.bfloat16)
    ends = jnp.cumsum(lengths[0])
    starts = ends - lengths[0]
    lane = jnp.arange(4, dtype=jnp.int32)[:, None]
    index = (lane * 4 + column % 4) * 128 + jnp.arange(128, dtype=jnp.int32)[None, :]
    inside = (index[..., None] >= starts) & (index[..., None] < ends)
    begin = jnp.sum(jnp.where(inside, starts, 0), -1)
    position = (index - begin).astype(jnp.float32)
    freqs = THETA_BASE ** (-jnp.arange(64, dtype=jnp.float32) * 2.0 / 128)
    angles = position[..., None] * freqs
    cosine, sine = jnp.cos(angles), jnp.sin(angles)
    cosf = jnp.concatenate([cosine, cosine], -1)
    sinf = jnp.concatenate([-sine, sine], -1)
    scale = math.log2(math.e) / math.sqrt(128)
    resid, moe_in, own_rows = attention_phase(
        normed, hidden, w_query, key_value_weight, w_out,
        (q_gain * scale).reshape(1, 128), key_norm_gain.reshape(1, 128),
        ffn_gain.reshape(1, 2048), cosf, sinf, begin[..., None],
    )
    logits = jnp.dot(moe_in, w_router, preferred_element_type=jnp.float32)
    soft_router = jax.nn.softmax(logits, -1)
    expert_count = w_router.shape[1]
    top_count = routes.shape[1]
    chosen = routes[:, :, None] == jnp.arange(expert_count, dtype=jnp.int32)[None, None, :]
    picked = jnp.sum(jnp.where(chosen, soft_router[:, None, :], 0.0), -1)
    gates = picked / jnp.sum(picked, 1, keepdims=True)
    capacity = 2 * tokens_here * top_count // expert_count
    flat_chosen = chosen.reshape(tokens_here * top_count, expert_count).astype(jnp.int32)
    ranks = jnp.cumsum(flat_chosen, 0) - 1
    slot_ids = jnp.sum(ranks * flat_chosen, 1)
    target = routes.reshape(-1) * capacity + slot_ids
    source_rows = moe_in[jnp.arange(tokens_here * top_count, dtype=jnp.int32) // top_count]
    send_rows = (
        jnp.zeros((expert_count * capacity, model_width), jnp.bfloat16).at[target].set(source_rows)
    )
    direct = send_rows.reshape(expert_count, capacity, model_width)
    batch = lax.all_to_all(direct, ("req", "exp"), split_axis=0, concat_axis=0, tiled=True)
    batch_shape = batch.shape
    rows_flat = batch.reshape(-1, batch_shape[-1])
    gate_part = jnp.dot(rows_flat, w_gate[0], preferred_element_type=jnp.float32)
    up_part = jnp.dot(rows_flat, w_up[0], preferred_element_type=jnp.float32)
    act = (jax.nn.silu(gate_part) * up_part).astype(jnp.bfloat16)
    answer = jnp.dot(act, w_down[0], preferred_element_type=jnp.float32).astype(jnp.bfloat16)
    answered = answer.reshape(batch_shape[:-1] + (w_down.shape[2],))
    returned = lax.all_to_all(answered, ("req", "exp"), split_axis=0, concat_axis=0, tiled=True)
    outcome = returned.reshape(expert_count * capacity, model_width)[target]
    outcome = outcome.reshape(tokens_here, top_count, model_width)
    moe_sum = jnp.sum(outcome.astype(jnp.float32) * gates[:, :, None], 1)
    layer_out = (resid.astype(jnp.float32) + moe_sum).astype(jnp.bfloat16)
    blocks_here = page_table.shape[0]
    page_size = tokens_here // blocks_here
    page_width = page_size * own_rows.shape[1]
    page_blocks = own_rows.reshape(blocks_here, page_width)
    req_count = lax.axis_size("req")
    per_peer = blocks_here // req_count
    owner = page_table // blocks_here // lax.axis_size("exp")
    owner_hit = (owner[:, None] == jnp.arange(req_count, dtype=jnp.int32)[None, :]).astype(
        jnp.int32
    )
    rank_inside = jnp.sum((jnp.cumsum(owner_hit, 0) - 1) * owner_hit, 1)
    send_order = owner * per_peer + rank_inside
    send_pages = jnp.zeros_like(page_blocks).at[send_order].set(page_blocks)
    send_slots = jnp.zeros_like(page_table).at[send_order].set(page_table % blocks_here)
    got_pages, got_slots = (
        lax.all_to_all(
            send_pages.reshape(req_count, per_peer, page_width),
            "req",
            split_axis=0,
            concat_axis=0,
            tiled=True,
        ),
        lax.all_to_all(
            send_slots.reshape(req_count, per_peer), "req", split_axis=0, concat_axis=0, tiled=True
        ),
    )
    kv_cache = (
        jnp.zeros_like(page_blocks)
        .at[got_slots.reshape(-1)]
        .set(got_pages.reshape(blocks_here, page_width))
    )
    return (layer_out, kv_cache)


def solution(mesh):
    in_specs = (
        P(("req", "exp"), None),
        P("req", None),
        P(),
        P(),
        P(),
        P(None, "exp"),
        P(),
        P("exp", None),
        P(),
        P(),
        P(("req", "exp"), None),
        P(("req", "exp"), None, None),
        P(("req", "exp"), None, None),
        P(("req", "exp"), None, None),
        P(("req", "exp")),
    )
    out_specs = (P(("req", "exp"), None), P(("req", "exp"), None))
    return jax.shard_map(
        on_device, mesh=mesh, in_specs=in_specs, out_specs=out_specs, check_vma=False
    )
```

```python
import functools
import math

import jax
import jax.numpy as jnp
from jax import lax
from jax.experimental import pallas as pl
from jax.experimental.pallas import tpu as pltpu
from jax.sharding import PartitionSpec as P

EPSILON = 1e-06
THETA_BASE = 1000000.0
MESH = pl.DeviceIdType.MESH
BF = jnp.bfloat16
F32 = jnp.float32


def rms_norm(values, scale_gain):
    values = values.astype(jnp.float32)
    factor = lax.rsqrt(jnp.mean(values * values, -1, keepdims=True) + EPSILON)
    return values * factor * scale_gain


def head_norm_rope(raw, gain, cosf, sinf):
    factor = lax.rsqrt(jnp.mean(raw * raw, -1, keepdims=True) + EPSILON)
    y = raw * factor * gain
    return y * cosf + pltpu.roll(y, 64, 1) * sinf


def attention_kernel(
    normed, hidden, wq, kvw, wo, q_gain, k_gain, ffn_gain, cosf, sinf, start,
    resid_o, moe_o, rows_o,
    tok, wqa, kvv, woa, ka, va, qs, ss, peak, acc, mixed, rs, part,
    lsem, tsend, trecv, wsend, wrecv, osend, orecv, ksend, krecv, rsend, rrecv,
):
    req = lax.axis_index("req")
    col = lax.axis_index("exp")
    z = col // 4
    x = col % 4
    core = req % 2

    def dz(d):
        return (req, lax.rem(z + d, 4) * 4 + x)

    def dx(d):
        return (req, z * 4 + lax.rem(x + d, 4))

    partner = (req + 1 - 2 * core, col)
    z1, z2, z3 = lax.rem(z + 1, 4), lax.rem(z + 2, 4), lax.rem(z + 3, 4)
    x1, x2, x3 = lax.rem(x + 1, 4), lax.rem(x + 2, 4), lax.rem(x + 3, 4)
    sent = []

    def orow(xx, off, size):
        return pl.ds(pl.multiple_of(xx * 256 + off, 64), size)

    def send(src, dst, ssem, rsem, dev):
        c = pltpu.make_async_remote_copy(
            src_ref=src, dst_ref=dst, send_sem=ssem, recv_sem=rsem,
            device_id=dev, device_id_type=MESH,
        )
        c.start()
        sent.append(c)

    def got(dst, rsem, ssem):
        pltpu.make_async_remote_copy(
            src_ref=dst, dst_ref=dst, send_sem=ssem, recv_sem=rsem,
            device_id=partner, device_id_type=MESH,
        ).wait_recv()

    local_kv = pltpu.make_async_copy(kvw, kvv, lsem.at[0])
    local_kv.start()
    local_wq = pltpu.make_async_copy(wq, wqa.at[x], lsem.at[1])
    local_wq.start()
    local_wo = pltpu.make_async_copy(wo, woa.at[orow(x, 0, 256)], lsem.at[2])
    local_wo.start()
    tok[z] = normed[...]
    va[:, 128:256] = jnp.ones((2048, 128), BF)

    barrier = pltpu.get_barrier_semaphore()
    for dev in (dz(1), dz(2), dz(3), dx(1), dx(3), partner):
        pl.semaphore_signal(barrier, inc=1, device_id=dev, device_id_type=MESH)
    pl.semaphore_wait(barrier, 6)

    send(normed, tok.at[z], tsend.at[0], trecv.at[0], dz(1))
    send(normed, tok.at[z], tsend.at[1], trecv.at[1], dz(3))
    half = core * 1024
    send(wq.at[pl.ds(half, 1024)], wqa.at[x, pl.ds(half, 1024)], wsend.at[0], wrecv.at[0], dx(1))
    send(wq.at[pl.ds(half, 1024)], wqa.at[x, pl.ds(half, 1024)], wsend.at[1], wrecv.at[1], dx(3))

    def krow(zz, xx):
        return pl.ds(pl.multiple_of((zz * 4 + xx) * 128, 128), 128)

    def send_kv(zz, j):
        rows = krow(zz, x)
        k = ka.at[rows]
        v = va.at[rows, pl.ds(0, 128)]
        send(k, k, ksend.at[j, 0], krecv.at[j, 0], dx(1))
        send(v, v, ksend.at[j, 1], krecv.at[j, 1], dx(1))
        send(k, k, ksend.at[j, 2], krecv.at[j, 2], dx(3))
        send(v, v, ksend.at[j, 3], krecv.at[j, 3], dx(3))

    def relay_kv(zz, j):
        left = krow(zz, x3)
        right = krow(zz, x1)
        k = ka.at[left]
        got(k, krecv.at[j, 0], ksend.at[j, 0])
        send(k, k, ksend.at[j, 4], krecv.at[j, 4], dx(1))
        v = va.at[right, pl.ds(0, 128)]
        got(v, krecv.at[j, 3], ksend.at[j, 3])
        send(v, v, ksend.at[j, 5], krecv.at[j, 5], dx(3))

    def finish_kv(zz, j):
        left = krow(zz, x3)
        right = krow(zz, x1)
        far = krow(zz, x2)
        got(va.at[left, pl.ds(0, 128)], krecv.at[j, 1], ksend.at[j, 1])
        got(ka.at[right], krecv.at[j, 2], ksend.at[j, 2])
        got(ka.at[far], krecv.at[j, 4], ksend.at[j, 4])
        got(va.at[far, pl.ds(0, 128)], krecv.at[j, 5], ksend.at[j, 5])

    local_kv.wait()
    own = jnp.dot(normed[...], kvv[...], preferred_element_type=F32)
    for h in range(4):
        rows_o[:, h * 128 : (h + 1) * 128] = head_norm_rope(
            own[:, h * 128 : (h + 1) * 128], k_gain[...], cosf[z], sinf[z]
        ).astype(BF)
    rows_o[:, 512:1024] = own[:, 512:1024].astype(BF)
    kcols = pl.ds(pl.multiple_of(z * 128, 128), 128)
    vcols = pl.ds(pl.multiple_of(512 + z * 128, 128), 128)
    ka[krow(z, x), :] = rows_o[:, kcols]
    va[krow(z, x), 0:128] = rows_o[:, vcols]
    send_kv(z, 0)

    def make_kv(zz):
        block = tok[zz]
        kk = jnp.dot(block, kvv[:, kcols], preferred_element_type=F32)
        vv = jnp.dot(block, kvv[:, vcols], preferred_element_type=F32)
        ka[krow(zz, x), :] = head_norm_rope(kk, k_gain[...], cosf[zz], sinf[zz]).astype(BF)
        va[krow(zz, x), 0:128] = vv.astype(BF)

    got(tok.at[z3], trecv.at[0], tsend.at[0])
    send(tok.at[z3, pl.ds(0, 64)], tok.at[z3, pl.ds(0, 64)], tsend.at[2], trecv.at[2], dz(1))
    got(tok.at[z1], trecv.at[1], tsend.at[1])
    send(tok.at[z1, pl.ds(64, 64)], tok.at[z1, pl.ds(64, 64)], tsend.at[3], trecv.at[3], dz(3))
    mine = pl.ds(half, 1024)
    got(wqa.at[x3, mine], wrecv.at[0], wsend.at[0])
    r0 = wqa.at[x3, pl.ds(half, 512)]
    send(r0, r0, wsend.at[2], wrecv.at[2], dx(1))
    got(wqa.at[x1, mine], wrecv.at[1], wsend.at[1])
    r1 = wqa.at[x1, pl.ds(half + 512, 512)]
    send(r1, r1, wsend.at[3], wrecv.at[3], dx(3))
    p0 = wqa.at[x3, mine]
    send(p0, p0, wsend.at[4], wrecv.at[4], partner)
    p1 = wqa.at[x1, mine]
    send(p1, p1, wsend.at[5], wrecv.at[5], partner)

    make_kv(z3)
    send_kv(z3, 1)
    make_kv(z1)
    send_kv(z1, 2)
    relay_kv(z, 0)
    ohalf = core * 128
    omine = pl.ds(ohalf, 128)
    send(wo.at[omine], woa.at[orow(x, ohalf, 128)], osend.at[0], orecv.at[0], dx(1))
    send(wo.at[omine], woa.at[orow(x, ohalf, 128)], osend.at[1], orecv.at[1], dx(3))
    got(tok.at[z2, pl.ds(0, 64)], trecv.at[2], tsend.at[2])
    got(tok.at[z2, pl.ds(64, 64)], trecv.at[3], tsend.at[3])
    make_kv(z2)
    send_kv(z2, 3)
    relay_kv(z3, 1)
    relay_kv(z1, 2)

    got(wqa.at[x2, pl.ds(half, 512)], wrecv.at[2], wsend.at[2])
    got(wqa.at[x2, pl.ds(half + 512, 512)], wrecv.at[3], wsend.at[3])
    p2 = wqa.at[x2, mine]
    send(p2, p2, wsend.at[6], wrecv.at[6], partner)
    local_wq.wait()

    def q_slice(xx):
        for zz in range(2):
            block = jnp.concatenate([tok[2 * zz], tok[2 * zz + 1]], 0)
            raw = jnp.dot(block, wqa[xx], preferred_element_type=F32)
            for b in range(2):
                for h in range(2):
                    y = head_norm_rope(
                        raw[b * 128 : (b + 1) * 128, h * 128 : (h + 1) * 128],
                        q_gain[...], cosf[2 * zz + b], sinf[2 * zz + b],
                    )
                    row = pl.ds(pl.multiple_of((xx * 2 + h) * 128, 128), 128)
                    qs[2 * zz + b, row, :] = y.astype(BF)

    q_slice(x)
    other = pl.ds(1024 - half, 1024)
    got(wqa.at[x3, other], wrecv.at[4], wsend.at[4])
    q_slice(x3)
    relay_kv(z2, 3)
    got(wqa.at[x1, other], wrecv.at[5], wsend.at[5])
    q_slice(x1)
    got(wqa.at[x2, other], wrecv.at[6], wsend.at[6])
    q_slice(x2)

    left_o = woa.at[orow(x3, ohalf, 128)]
    right_o = woa.at[orow(x1, ohalf, 128)]
    far_o = woa.at[orow(x2, ohalf, 128)]
    got(left_o, orecv.at[0], osend.at[0])
    o0 = woa.at[orow(x3, ohalf, 64)]
    send(o0, o0, osend.at[2], orecv.at[2], dx(1))
    got(right_o, orecv.at[1], osend.at[1])
    o1 = woa.at[orow(x1, ohalf + 64, 64)]
    send(o1, o1, osend.at[3], orecv.at[3], dx(3))
    send(left_o, left_o, osend.at[4], orecv.at[4], partner)
    send(right_o, right_o, osend.at[5], orecv.at[5], partner)
    for zz, j in ((z, 0), (z3, 1), (z1, 2), (z2, 3)):
        finish_kv(zz, j)
    last_o = pltpu.make_async_remote_copy(
        src_ref=far_o, dst_ref=far_o, send_sem=osend.at[6], recv_sem=orecv.at[6],
        device_id=partner, device_id_type=MESH,
    )

    def attend(b):
        low = start[b]
        here = (b * 4 + x) * 128 + lax.broadcasted_iota(jnp.int32, (128, 512), 0)
        peak[...] = jnp.full((1024, 128), -1e30, F32)

        def score_step(c, carry):
            keys = pl.ds(pl.multiple_of(c * 512, 512), 512)
            s = lax.dot_general(
                qs[b], ka[keys, :], (((1,), (1,)), ((), ())), preferred_element_type=F32
            )
            kid = c * 512 + lax.broadcasted_iota(jnp.int32, (128, 512), 1)
            bias = jnp.where((kid >= low) & (kid <= here), 0.0, -1e30)
            s = (s.reshape(8, 128, 512) + bias[None]).reshape(1024, 512)
            ss[:, keys] = s
            top = peak[...]
            for g in range(4):
                top = jnp.maximum(top, s[:, g * 128 : (g + 1) * 128])
            peak[...] = top
            return carry

        lax.fori_loop(0, b + 1, score_step, 0)
        peak[...] = jnp.broadcast_to(jnp.max(peak[...], -1, keepdims=True), (1024, 128))
        acc[...] = jnp.zeros((1024, 256), F32)

        def mix_step(c, carry):
            keys = pl.ds(pl.multiple_of(c * 512, 512), 512)
            p = jnp.exp2(ss[:, keys] - peak[:, 0:1]).astype(BF)
            acc[...] += jnp.dot(p, va[keys, :], preferred_element_type=F32)
            return carry

        lax.fori_loop(0, b + 1, mix_step, 0)
        for h in range(8):
            rows = slice(h * 128, (h + 1) * 128)
            mixed[:, h * 128 : (h + 1) * 128] = (acc[rows, 0:128] / acc[rows, 128:256]).astype(BF)

    def share(i, off):
        b = lax.rem(z + off, 4)
        return pltpu.make_async_remote_copy(
            src_ref=part.at[b], dst_ref=rs.at[z], send_sem=rsend.at[i], recv_sem=rrecv.at[i],
            device_id=(req, b * 4 + x), device_id_type=MESH,
        )

    def block_step(i, carry):
        off = jnp.where(i == 0, 2, jnp.where(i == 1, 1, jnp.where(i == 2, 3, 0)))
        b = lax.rem(z + off, 4)
        attend(b)

        @pl.when(i == 0)
        def _():
            got(woa.at[orow(x2, ohalf, 64)], orecv.at[2], osend.at[2])
            got(woa.at[orow(x2, ohalf + 64, 64)], orecv.at[3], osend.at[3])
            last_o.start()
            got(woa.at[orow(x3, 128 - ohalf, 128)], orecv.at[4], osend.at[4])
            got(woa.at[orow(x1, 128 - ohalf, 128)], orecv.at[5], osend.at[5])
            got(woa.at[orow(x2, 128 - ohalf, 128)], orecv.at[6], osend.at[6])
            local_wo.wait()

        for n in range(2):
            cols = slice(n * 1024, (n + 1) * 1024)
            part[b, :, cols] = jnp.dot(
                mixed[...], woa[:, cols], preferred_element_type=F32
            ).astype(BF)

        @pl.when(i < 3)
        def _():
            share(i, off).start()

        return carry

    lax.fori_loop(0, 4, block_step, 0)
    for i, off in enumerate((2, 1, 3)):
        src = lax.rem(z + 4 - off, 4)
        got(rs.at[src], rrecv.at[i], rsend.at[i])
    total = hidden[...].astype(F32) + part[z].astype(F32)
    for d in range(1, 4):
        total = total + rs[lax.rem(z + d, 4)].astype(F32)
    resid = total.astype(BF)
    resid_o[...] = resid
    rf = resid.astype(F32)
    factor = lax.rsqrt(jnp.mean(rf * rf, -1, keepdims=True) + EPSILON)
    moe_o[...] = (rf * factor * ffn_gain[...]).astype(BF)
    for c in sent:
        c.wait_send()
    last_o.wait_send()
    for i, off in enumerate((2, 1, 3)):
        share(i, off).wait_send()


def attention_phase(normed, hidden, w_query, key_value_weight, w_out, q_gain, k_gain, ffn_gain, cosf, sinf, start):
    vmem = pl.BlockSpec(memory_space=pltpu.VMEM)
    hbm = pl.BlockSpec(memory_space=pl.ANY)
    dma = pltpu.SemaphoreType.DMA
    return pl.pallas_call(
        attention_kernel,
        name="attention",
        out_shape=(
            jax.ShapeDtypeStruct((128, 2048), BF),
            jax.ShapeDtypeStruct((128, 2048), BF),
            jax.ShapeDtypeStruct((128, 1024), BF),
        ),
        in_specs=[vmem, vmem, hbm, hbm, hbm, vmem, vmem, vmem, vmem, vmem, vmem],
        out_specs=(vmem, vmem, vmem),
        scratch_shapes=[
            pltpu.VMEM((4, 128, 2048), BF),
            pltpu.VMEM((4, 2048, 256), BF),
            pltpu.VMEM((2048, 1024), BF),
            pltpu.VMEM((1024, 2048), BF),
            pltpu.VMEM((2048, 128), BF),
            pltpu.VMEM((2048, 256), BF),
            pltpu.VMEM((4, 1024, 128), BF),
            pltpu.VMEM((1024, 2048), F32),
            pltpu.VMEM((1024, 128), F32),
            pltpu.VMEM((1024, 256), F32),
            pltpu.VMEM((128, 1024), BF),
            pltpu.VMEM((4, 128, 2048), BF),
            pltpu.VMEM((4, 128, 2048), BF),
            dma((3,)), dma((4,)), dma((4,)), dma((7,)), dma((7,)), dma((7,)), dma((7,)),
            dma((4, 6)), dma((4, 6)), dma((3,)), dma((3,)),
        ],
        compiler_params=pltpu.CompilerParams(
            collective_id=0, has_side_effects=True, vmem_limit_bytes=60 * 1024 * 1024
        ),
    )(normed, hidden, w_query, key_value_weight, w_out, q_gain, k_gain, ffn_gain, cosf, sinf, start)


def on_device(
    hidden,
    lengths,
    attn_gain,
    q_gain,
    key_norm_gain,
    w_query,
    key_value_weight,
    w_out,
    ffn_gain,
    w_router,
    routes,
    w_gate,
    w_up,
    w_down,
    page_table,
):
    column = lax.axis_index("exp")
    tokens_here = hidden.shape[0]
    model_width = hidden.shape[1]
    normed = rms_norm(hidden, attn_gain).astype(jnp.bfloat16)
    ends = jnp.cumsum(lengths[0])
    starts = ends - lengths[0]
    lane = jnp.arange(4, dtype=jnp.int32)[:, None]
    index = (lane * 4 + column % 4) * 128 + jnp.arange(128, dtype=jnp.int32)[None, :]
    inside = (index[..., None] >= starts) & (index[..., None] < ends)
    begin = jnp.sum(jnp.where(inside, starts, 0), -1)
    position = (index - begin).astype(jnp.float32)
    freqs = THETA_BASE ** (-jnp.arange(64, dtype=jnp.float32) * 2.0 / 128)
    angles = position[..., None] * freqs
    cosine, sine = jnp.cos(angles), jnp.sin(angles)
    cosf = jnp.concatenate([cosine, cosine], -1)
    sinf = jnp.concatenate([-sine, sine], -1)
    scale = math.log2(math.e) / math.sqrt(128)
    resid, moe_in, own_rows = attention_phase(
        normed, hidden, w_query, key_value_weight, w_out,
        (q_gain * scale).reshape(1, 128), key_norm_gain.reshape(1, 128),
        ffn_gain.reshape(1, 2048), cosf, sinf, begin[..., None],
    )
    logits = jnp.dot(moe_in, w_router, preferred_element_type=jnp.float32)
    soft_router = jax.nn.softmax(logits, -1)
    expert_count = w_router.shape[1]
    top_count = routes.shape[1]
    capacity = 2 * tokens_here * top_count // expert_count
    experts = jnp.arange(expert_count, dtype=jnp.int32)
    chosen = jnp.any(routes[:, None, :] == experts[None, :, None], -1)
    weights = jnp.where(chosen, soft_router, 0.0)
    gates = weights / jnp.sum(weights, 1, keepdims=True)
    token = jnp.arange(tokens_here, dtype=jnp.int32)
    earlier = (token[:, None] < token[None, :]).astype(BF)
    chosen_t = chosen.T
    ranks = jnp.dot(chosen_t.astype(BF), earlier, preferred_element_type=F32).astype(jnp.int32)
    slot = jnp.arange(capacity, dtype=jnp.int32)
    placed = chosen_t[:, None, :] & (ranks[:, None, :] == slot[None, :, None])
    place = placed.astype(BF).reshape(expert_count * capacity, tokens_here)
    send_rows = jnp.dot(place, moe_in, preferred_element_type=F32).astype(BF)
    direct = send_rows.reshape(expert_count, capacity, model_width)
    batch = lax.all_to_all(direct, ("req", "exp"), split_axis=0, concat_axis=0, tiled=True)
    batch_shape = batch.shape
    rows_flat = batch.reshape(-1, batch_shape[-1])
    gate_part = jnp.dot(rows_flat, w_gate[0], preferred_element_type=jnp.float32)
    up_part = jnp.dot(rows_flat, w_up[0], preferred_element_type=jnp.float32)
    act = (jax.nn.silu(gate_part) * up_part).astype(jnp.bfloat16)
    answer = jnp.dot(act, w_down[0], preferred_element_type=jnp.float32).astype(jnp.bfloat16)
    answered = answer.reshape(batch_shape[:-1] + (w_down.shape[2],))
    returned = lax.all_to_all(answered, ("req", "exp"), split_axis=0, concat_axis=0, tiled=True)
    spread = jnp.where(placed, gates.T[:, None, :], 0.0).reshape(-1, tokens_here)
    high = lax.reduce_precision(spread, 8, 7)
    both = jnp.concatenate([high.astype(BF), (spread - high).astype(BF)], 1)
    sums = lax.dot_general(
        both, returned.reshape(-1, model_width), (((0,), (0,)), ((), ())),
        preferred_element_type=F32,
    )
    moe_sum = sums[:tokens_here] + sums[tokens_here:]
    layer_out = (resid.astype(jnp.float32) + moe_sum).astype(jnp.bfloat16)
    blocks_here = page_table.shape[0]
    page_size = tokens_here // blocks_here
    page_width = page_size * own_rows.shape[1]
    page_blocks = own_rows.reshape(blocks_here, page_width)
    req_count = lax.axis_size("req")
    per_peer = blocks_here // req_count
    owner = page_table // blocks_here // lax.axis_size("exp")
    owner_hit = (owner[:, None] == jnp.arange(req_count, dtype=jnp.int32)[None, :]).astype(
        jnp.int32
    )
    rank_inside = jnp.sum((jnp.cumsum(owner_hit, 0) - 1) * owner_hit, 1)
    send_order = owner * per_peer + rank_inside
    send_pages = jnp.zeros_like(page_blocks).at[send_order].set(page_blocks)
    send_slots = jnp.zeros_like(page_table).at[send_order].set(page_table % blocks_here)
    got_pages, got_slots = (
        lax.all_to_all(
            send_pages.reshape(req_count, per_peer, page_width),
            "req",
            split_axis=0,
            concat_axis=0,
            tiled=True,
        ),
        lax.all_to_all(
            send_slots.reshape(req_count, per_peer), "req", split_axis=0, concat_axis=0, tiled=True
        ),
    )
    kv_cache = (
        jnp.zeros_like(page_blocks)
        .at[got_slots.reshape(-1)]
        .set(got_pages.reshape(blocks_here, page_width))
    )
    return (layer_out, kv_cache)


def solution(mesh):
    in_specs = (
        P(("req", "exp"), None),
        P("req", None),
        P(),
        P(),
        P(),
        P(None, "exp"),
        P(),
        P("exp", None),
        P(),
        P(),
        P(("req", "exp"), None),
        P(("req", "exp"), None, None),
        P(("req", "exp"), None, None),
        P(("req", "exp"), None, None),
        P(("req", "exp")),
    )
    out_specs = (P(("req", "exp"), None), P(("req", "exp"), None))
    return jax.shard_map(
        on_device, mesh=mesh, in_specs=in_specs, out_specs=out_specs, check_vma=False
    )
```

```python
import functools
import math

import jax
import jax.numpy as jnp
from jax import lax
from jax.experimental import pallas as pl
from jax.experimental.pallas import tpu as pltpu
from jax.sharding import PartitionSpec as P

EPSILON = 1e-06
THETA_BASE = 1000000.0
MESH = pl.DeviceIdType.MESH
BF = jnp.bfloat16
F32 = jnp.float32


def rms_norm(values, scale_gain):
    values = values.astype(jnp.float32)
    factor = lax.rsqrt(jnp.mean(values * values, -1, keepdims=True) + EPSILON)
    return values * factor * scale_gain


def head_norm_rope(raw, gain, cosf, sinf):
    factor = lax.rsqrt(jnp.mean(raw * raw, -1, keepdims=True) + EPSILON)
    y = raw * factor * gain
    return y * cosf + pltpu.roll(y, 64, 1) * sinf


def attention_kernel(
    normed, hidden, wq, kvw, wo, q_gain, k_gain, ffn_gain, cosf, sinf, start,
    resid_o, moe_o, rows_o,
    tok, wqa, kvv, woa, ka, va, qs, ss, peak, acc, mixed, rs, part,
    lsem, tsend, trecv, wsend, wrecv, osend, orecv, ksend, krecv, rsend, rrecv,
):
    req = lax.axis_index("req")
    col = lax.axis_index("exp")
    z = col // 4
    x = col % 4
    core = req % 2

    def dz(d):
        return (req, lax.rem(z + d, 4) * 4 + x)

    def dx(d):
        return (req, z * 4 + lax.rem(x + d, 4))

    partner = (req + 1 - 2 * core, col)
    z1, z2, z3 = lax.rem(z + 1, 4), lax.rem(z + 2, 4), lax.rem(z + 3, 4)
    x1, x2, x3 = lax.rem(x + 1, 4), lax.rem(x + 2, 4), lax.rem(x + 3, 4)
    sent = []

    def orow(xx, off, size):
        return pl.ds(pl.multiple_of(xx * 256 + off, 64), size)

    def send(src, dst, ssem, rsem, dev):
        c = pltpu.make_async_remote_copy(
            src_ref=src, dst_ref=dst, send_sem=ssem, recv_sem=rsem,
            device_id=dev, device_id_type=MESH,
        )
        c.start()
        sent.append(c)

    def got(dst, rsem, ssem):
        pltpu.make_async_remote_copy(
            src_ref=dst, dst_ref=dst, send_sem=ssem, recv_sem=rsem,
            device_id=partner, device_id_type=MESH,
        ).wait_recv()

    local_kv = pltpu.make_async_copy(kvw, kvv, lsem.at[0])
    local_kv.start()
    local_wq = pltpu.make_async_copy(wq, wqa.at[x], lsem.at[1])
    local_wq.start()
    local_wo = pltpu.make_async_copy(wo, woa.at[orow(x, 0, 256)], lsem.at[2])
    local_wo.start()
    tok[z] = normed[...]
    va[:, 128:256] = jnp.ones((2048, 128), BF)

    barrier = pltpu.get_barrier_semaphore()
    for dev in (dz(1), dz(2), dz(3), dx(1), dx(3), partner):
        pl.semaphore_signal(barrier, inc=1, device_id=dev, device_id_type=MESH)
    pl.semaphore_wait(barrier, 6)

    send(normed, tok.at[z], tsend.at[0], trecv.at[0], dz(1))
    send(normed, tok.at[z], tsend.at[1], trecv.at[1], dz(3))
    half = core * 1024
    send(wq.at[pl.ds(half, 1024)], wqa.at[x, pl.ds(half, 1024)], wsend.at[0], wrecv.at[0], dx(1))
    send(wq.at[pl.ds(half, 1024)], wqa.at[x, pl.ds(half, 1024)], wsend.at[1], wrecv.at[1], dx(3))

    def krow(zz, xx):
        return pl.ds(pl.multiple_of((zz * 4 + xx) * 128, 128), 128)

    def send_kv(zz, j):
        rows = krow(zz, x)
        k = ka.at[rows]
        v = va.at[rows, pl.ds(0, 128)]
        send(k, k, ksend.at[j, 0], krecv.at[j, 0], dx(1))
        send(v, v, ksend.at[j, 1], krecv.at[j, 1], dx(1))
        send(k, k, ksend.at[j, 2], krecv.at[j, 2], dx(3))
        send(v, v, ksend.at[j, 3], krecv.at[j, 3], dx(3))

    def relay_kv(zz, j):
        left = krow(zz, x3)
        right = krow(zz, x1)
        k = ka.at[left]
        got(k, krecv.at[j, 0], ksend.at[j, 0])
        send(k, k, ksend.at[j, 4], krecv.at[j, 4], dx(1))
        v = va.at[right, pl.ds(0, 128)]
        got(v, krecv.at[j, 3], ksend.at[j, 3])
        send(v, v, ksend.at[j, 5], krecv.at[j, 5], dx(3))

    def finish_kv(zz, j):
        left = krow(zz, x3)
        right = krow(zz, x1)
        far = krow(zz, x2)
        got(va.at[left, pl.ds(0, 128)], krecv.at[j, 1], ksend.at[j, 1])
        got(ka.at[right], krecv.at[j, 2], ksend.at[j, 2])
        got(ka.at[far], krecv.at[j, 4], ksend.at[j, 4])
        got(va.at[far, pl.ds(0, 128)], krecv.at[j, 5], ksend.at[j, 5])

    local_kv.wait()
    own = jnp.dot(normed[...], kvv[...], preferred_element_type=F32)
    for h in range(4):
        rows_o[:, h * 128 : (h + 1) * 128] = head_norm_rope(
            own[:, h * 128 : (h + 1) * 128], k_gain[...], cosf[z], sinf[z]
        ).astype(BF)
    rows_o[:, 512:1024] = own[:, 512:1024].astype(BF)
    kcols = pl.ds(pl.multiple_of(z * 128, 128), 128)
    vcols = pl.ds(pl.multiple_of(512 + z * 128, 128), 128)
    ka[krow(z, x), :] = rows_o[:, kcols]
    va[krow(z, x), 0:128] = rows_o[:, vcols]
    send_kv(z, 0)

    def make_kv(zz):
        block = tok[zz]
        kk = jnp.dot(block, kvv[:, kcols], preferred_element_type=F32)
        vv = jnp.dot(block, kvv[:, vcols], preferred_element_type=F32)
        ka[krow(zz, x), :] = head_norm_rope(kk, k_gain[...], cosf[zz], sinf[zz]).astype(BF)
        va[krow(zz, x), 0:128] = vv.astype(BF)

    got(tok.at[z3], trecv.at[0], tsend.at[0])
    send(tok.at[z3, pl.ds(0, 64)], tok.at[z3, pl.ds(0, 64)], tsend.at[2], trecv.at[2], dz(1))
    got(tok.at[z1], trecv.at[1], tsend.at[1])
    send(tok.at[z1, pl.ds(64, 64)], tok.at[z1, pl.ds(64, 64)], tsend.at[3], trecv.at[3], dz(3))
    mine = pl.ds(half, 1024)
    got(wqa.at[x3, mine], wrecv.at[0], wsend.at[0])
    r0 = wqa.at[x3, pl.ds(half, 512)]
    send(r0, r0, wsend.at[2], wrecv.at[2], dx(1))
    got(wqa.at[x1, mine], wrecv.at[1], wsend.at[1])
    r1 = wqa.at[x1, pl.ds(half + 512, 512)]
    send(r1, r1, wsend.at[3], wrecv.at[3], dx(3))
    p0 = wqa.at[x3, mine]
    send(p0, p0, wsend.at[4], wrecv.at[4], partner)
    p1 = wqa.at[x1, mine]
    send(p1, p1, wsend.at[5], wrecv.at[5], partner)

    make_kv(z3)
    send_kv(z3, 1)
    make_kv(z1)
    send_kv(z1, 2)
    relay_kv(z, 0)
    ohalf = core * 128
    omine = pl.ds(ohalf, 128)
    send(wo.at[omine], woa.at[orow(x, ohalf, 128)], osend.at[0], orecv.at[0], dx(1))
    send(wo.at[omine], woa.at[orow(x, ohalf, 128)], osend.at[1], orecv.at[1], dx(3))
    got(tok.at[z2, pl.ds(0, 64)], trecv.at[2], tsend.at[2])
    got(tok.at[z2, pl.ds(64, 64)], trecv.at[3], tsend.at[3])
    make_kv(z2)
    send_kv(z2, 3)
    relay_kv(z3, 1)
    relay_kv(z1, 2)

    got(wqa.at[x2, pl.ds(half, 512)], wrecv.at[2], wsend.at[2])
    got(wqa.at[x2, pl.ds(half + 512, 512)], wrecv.at[3], wsend.at[3])
    p2 = wqa.at[x2, mine]
    send(p2, p2, wsend.at[6], wrecv.at[6], partner)
    local_wq.wait()

    def q_slice(xx):
        for zz in range(2):
            block = jnp.concatenate([tok[2 * zz], tok[2 * zz + 1]], 0)
            raw = jnp.dot(block, wqa[xx], preferred_element_type=F32)
            for b in range(2):
                for h in range(2):
                    y = head_norm_rope(
                        raw[b * 128 : (b + 1) * 128, h * 128 : (h + 1) * 128],
                        q_gain[...], cosf[2 * zz + b], sinf[2 * zz + b],
                    )
                    row = pl.ds(pl.multiple_of((xx * 2 + h) * 128, 128), 128)
                    qs[2 * zz + b, row, :] = y.astype(BF)

    q_slice(x)
    other = pl.ds(1024 - half, 1024)
    got(wqa.at[x3, other], wrecv.at[4], wsend.at[4])
    q_slice(x3)
    relay_kv(z2, 3)
    got(wqa.at[x1, other], wrecv.at[5], wsend.at[5])
    q_slice(x1)
    got(wqa.at[x2, other], wrecv.at[6], wsend.at[6])
    q_slice(x2)

    left_o = woa.at[orow(x3, ohalf, 128)]
    right_o = woa.at[orow(x1, ohalf, 128)]
    far_o = woa.at[orow(x2, ohalf, 128)]
    got(left_o, orecv.at[0], osend.at[0])
    o0 = woa.at[orow(x3, ohalf, 64)]
    send(o0, o0, osend.at[2], orecv.at[2], dx(1))
    got(right_o, orecv.at[1], osend.at[1])
    o1 = woa.at[orow(x1, ohalf + 64, 64)]
    send(o1, o1, osend.at[3], orecv.at[3], dx(3))
    send(left_o, left_o, osend.at[4], orecv.at[4], partner)
    send(right_o, right_o, osend.at[5], orecv.at[5], partner)
    for zz, j in ((z, 0), (z3, 1), (z1, 2), (z2, 3)):
        finish_kv(zz, j)
    last_o = pltpu.make_async_remote_copy(
        src_ref=far_o, dst_ref=far_o, send_sem=osend.at[6], recv_sem=orecv.at[6],
        device_id=partner, device_id_type=MESH,
    )

    def attend(b):
        low = start[b]
        here = (b * 4 + x) * 128 + lax.broadcasted_iota(jnp.int32, (128, 512), 0)
        peak[...] = jnp.full((1024, 128), -1e30, F32)

        def score_step(c, carry):
            keys = pl.ds(pl.multiple_of(c * 512, 512), 512)
            s = lax.dot_general(
                qs[b], ka[keys, :], (((1,), (1,)), ((), ())), preferred_element_type=F32
            )
            kid = c * 512 + lax.broadcasted_iota(jnp.int32, (128, 512), 1)
            bias = jnp.where((kid >= low) & (kid <= here), 0.0, -1e30)
            s = (s.reshape(8, 128, 512) + bias[None]).reshape(1024, 512)
            ss[:, keys] = s
            top = peak[...]
            for g in range(4):
                top = jnp.maximum(top, s[:, g * 128 : (g + 1) * 128])
            peak[...] = top
            return carry

        lax.fori_loop(0, b + 1, score_step, 0)
        peak[...] = jnp.broadcast_to(jnp.max(peak[...], -1, keepdims=True), (1024, 128))
        acc[...] = jnp.zeros((1024, 256), F32)

        def mix_step(c, carry):
            keys = pl.ds(pl.multiple_of(c * 512, 512), 512)
            p = jnp.exp2(ss[:, keys] - peak[:, 0:1]).astype(BF)
            acc[...] += jnp.dot(p, va[keys, :], preferred_element_type=F32)
            return carry

        lax.fori_loop(0, b + 1, mix_step, 0)
        for h in range(8):
            rows = slice(h * 128, (h + 1) * 128)
            mixed[:, h * 128 : (h + 1) * 128] = (acc[rows, 0:128] / acc[rows, 128:256]).astype(BF)

    def share(i, off):
        b = lax.rem(z + off, 4)
        return pltpu.make_async_remote_copy(
            src_ref=part.at[b], dst_ref=rs.at[z], send_sem=rsend.at[i], recv_sem=rrecv.at[i],
            device_id=(req, b * 4 + x), device_id_type=MESH,
        )

    def block_step(i, carry):
        off = jnp.where(i == 0, 2, jnp.where(i == 1, 1, jnp.where(i == 2, 3, 0)))
        b = lax.rem(z + off, 4)
        attend(b)

        @pl.when(i == 0)
        def _():
            got(woa.at[orow(x2, ohalf, 64)], orecv.at[2], osend.at[2])
            got(woa.at[orow(x2, ohalf + 64, 64)], orecv.at[3], osend.at[3])
            last_o.start()
            got(woa.at[orow(x3, 128 - ohalf, 128)], orecv.at[4], osend.at[4])
            got(woa.at[orow(x1, 128 - ohalf, 128)], orecv.at[5], osend.at[5])
            got(woa.at[orow(x2, 128 - ohalf, 128)], orecv.at[6], osend.at[6])
            local_wo.wait()

        for n in range(2):
            cols = slice(n * 1024, (n + 1) * 1024)
            part[b, :, cols] = jnp.dot(
                mixed[...], woa[:, cols], preferred_element_type=F32
            ).astype(BF)

        @pl.when(i < 3)
        def _():
            share(i, off).start()

        return carry

    lax.fori_loop(0, 4, block_step, 0)
    for i, off in enumerate((2, 1, 3)):
        src = lax.rem(z + 4 - off, 4)
        got(rs.at[src], rrecv.at[i], rsend.at[i])
    total = hidden[...].astype(F32) + part[z].astype(F32)
    for d in range(1, 4):
        total = total + rs[lax.rem(z + d, 4)].astype(F32)
    resid = total.astype(BF)
    resid_o[...] = resid
    rf = resid.astype(F32)
    factor = lax.rsqrt(jnp.mean(rf * rf, -1, keepdims=True) + EPSILON)
    moe_o[...] = (rf * factor * ffn_gain[...]).astype(BF)
    for c in sent:
        c.wait_send()
    last_o.wait_send()
    for i, off in enumerate((2, 1, 3)):
        share(i, off).wait_send()


def attention_phase(normed, hidden, w_query, key_value_weight, w_out, q_gain, k_gain, ffn_gain, cosf, sinf, start):
    vmem = pl.BlockSpec(memory_space=pltpu.VMEM)
    hbm = pl.BlockSpec(memory_space=pl.ANY)
    dma = pltpu.SemaphoreType.DMA
    return pl.pallas_call(
        attention_kernel,
        name="attention",
        out_shape=(
            jax.ShapeDtypeStruct((128, 2048), BF),
            jax.ShapeDtypeStruct((128, 2048), BF),
            jax.ShapeDtypeStruct((128, 1024), BF),
        ),
        in_specs=[vmem, vmem, hbm, hbm, hbm, vmem, vmem, vmem, vmem, vmem, vmem],
        out_specs=(vmem, vmem, vmem),
        scratch_shapes=[
            pltpu.VMEM((4, 128, 2048), BF),
            pltpu.VMEM((4, 2048, 256), BF),
            pltpu.VMEM((2048, 1024), BF),
            pltpu.VMEM((1024, 2048), BF),
            pltpu.VMEM((2048, 128), BF),
            pltpu.VMEM((2048, 256), BF),
            pltpu.VMEM((4, 1024, 128), BF),
            pltpu.VMEM((1024, 2048), F32),
            pltpu.VMEM((1024, 128), F32),
            pltpu.VMEM((1024, 256), F32),
            pltpu.VMEM((128, 1024), BF),
            pltpu.VMEM((4, 128, 2048), BF),
            pltpu.VMEM((4, 128, 2048), BF),
            dma((3,)), dma((4,)), dma((4,)), dma((7,)), dma((7,)), dma((7,)), dma((7,)),
            dma((4, 6)), dma((4, 6)), dma((3,)), dma((3,)),
        ],
        compiler_params=pltpu.CompilerParams(
            collective_id=0, has_side_effects=True, vmem_limit_bytes=60 * 1024 * 1024
        ),
    )(normed, hidden, w_query, key_value_weight, w_out, q_gain, k_gain, ffn_gain, cosf, sinf, start)


def offset_parts(i):
    chunk = lax.div(i, 16)
    inner = lax.rem(i, 16)
    oy, oz = lax.div(inner, 4), lax.rem(inner, 4)
    ox = lax.rem(lax.rem(chunk, 4) + 8 - oy - oz, 4)
    return oy, lax.div(chunk, 4), oz, ox


def experts_kernel(
    moe, resid, place, place_t, chosen, router, wg, wu, wd,
    out,
    rows, batch, answers, back, wgv, wuv, wdv, acc,
    lsem, dsend, drecv, asend, arecv,
):
    req = lax.axis_index("req")
    col = lax.axis_index("exp")
    y, core = lax.div(req, 2), lax.rem(req, 2)
    z, x = lax.div(col, 4), lax.rem(col, 4)

    def target(i):
        oy, oc, oz, ox = offset_parts(i)
        return (
            lax.rem(y + oy, 4) * 2 + core + oc - 2 * core * oc,
            lax.rem(z + oz, 4) * 4 + lax.rem(x + ox, 4),
        )

    def origin(i):
        oy, oc, oz, ox = offset_parts(i)
        return (
            lax.rem(y + 4 - oy, 4) * 2 + core + oc - 2 * core * oc,
            lax.rem(z + 4 - oz, 4) * 4 + lax.rem(x + 4 - ox, 4),
        )

    loads = [
        pltpu.make_async_copy(src.at[0], dst, lsem.at[n])
        for n, (src, dst) in enumerate(((wg, wgv), (wu, wuv), (wd, wdv)))
    ]
    for c in loads:
        c.start()

    barrier = pltpu.get_barrier_semaphore()

    def greet(i, carry):
        pl.semaphore_signal(barrier, inc=1, device_id=target(i), device_id_type=MESH)
        return carry

    lax.fori_loop(1, 128, greet, 0)

    def chunk_rows(j):
        return pl.ds(pl.multiple_of(j * 256, 256), 256)

    def build(j, carry):
        r = chunk_rows(j)
        rows[r, :] = jnp.dot(place[r, :], moe[...], preferred_element_type=F32).astype(BF)
        return carry

    lax.fori_loop(0, 8, build, 0)
    batch[0:16, :] = rows[0:16, :]
    pl.semaphore_wait(barrier, 127)

    def dispatch(i, carry):
        r = pl.ds(pl.multiple_of(i * 16, 16), 16)
        pltpu.make_async_remote_copy(
            src_ref=rows.at[r], dst_ref=batch.at[r],
            send_sem=dsend.at[lax.div(i, 16)], recv_sem=drecv.at[lax.div(i, 16)],
            device_id=target(i), device_id_type=MESH,
        ).start()
        return carry

    lax.fori_loop(1, 128, dispatch, 0)

    def whole(buf, ssem, rsem, j, r):
        return pltpu.make_async_remote_copy(
            src_ref=buf.at[r], dst_ref=buf.at[r], send_sem=ssem.at[j], recv_sem=rsem.at[j],
            device_id=target(1), device_id_type=MESH,
        )

    def arrived(buf, ssem, rsem, j):
        @pl.when(j == 0)
        def _():
            whole(buf, ssem, rsem, j, pl.ds(16, 240)).wait_recv()

        @pl.when(j > 0)
        def _():
            whole(buf, ssem, rsem, j, chunk_rows(j)).wait_recv()

    def left(buf, ssem, rsem, j):
        @pl.when(j == 0)
        def _():
            whole(buf, ssem, rsem, j, pl.ds(16, 240)).wait_send()

        @pl.when(j > 0)
        def _():
            whole(buf, ssem, rsem, j, chunk_rows(j)).wait_send()

    logits = jnp.dot(moe[...], router[...], preferred_element_type=F32)
    grown = jnp.exp(logits - jnp.max(logits, -1, keepdims=True))
    soft = grown / jnp.sum(grown, -1, keepdims=True)
    picked = soft * chosen[...]
    gates = picked / jnp.sum(picked, -1, keepdims=True)
    high = gates.astype(BF)
    low = (gates - high.astype(F32)).astype(BF)
    both = jnp.concatenate([high, low], 0)
    acc[...] = jnp.zeros((256, 2048), F32)
    for c in loads:
        c.wait()

    def work(j, carry):
        arrived(batch, dsend, drecv, j)
        r = chunk_rows(j)
        taken = batch[r, :]
        g = jnp.dot(taken, wgv[...], preferred_element_type=F32)
        u = jnp.dot(taken, wuv[...], preferred_element_type=F32)
        act = (g / (1.0 + jnp.exp(-g)) * u).astype(BF)
        answers[r, :] = jnp.dot(act, wdv[...], preferred_element_type=F32).astype(BF)

        def reply(q, inner):
            i = j * 16 + q
            p = pl.ds(pl.multiple_of(i * 16, 16), 16)
            pltpu.make_async_remote_copy(
                src_ref=answers.at[p], dst_ref=back.at[p],
                send_sem=asend.at[j], recv_sem=arecv.at[j],
                device_id=origin(i), device_id_type=MESH,
            ).start()
            return inner

        @pl.when(j == 0)
        def _():
            back[0:16, :] = answers[0:16, :]
            lax.fori_loop(1, 16, reply, 0)

        @pl.when(j > 0)
        def _():
            lax.fori_loop(0, 16, reply, 0)

        return carry

    lax.fori_loop(0, 8, work, 0)

    def combine(j, carry):
        arrived(back, asend, arecv, j)
        r = chunk_rows(j)
        expert = lax.broadcasted_iota(jnp.int32, (128, 256), 0)
        owner = j * 16 + lax.broadcasted_iota(jnp.int32, (128, 256), 1) // 16
        pick = jnp.where(expert == owner, 1.0, 0.0).astype(BF)
        spread = jnp.dot(both, pick, preferred_element_type=F32)
        mask = place_t[:, r].astype(F32)
        spread = (spread.reshape(2, 128, 256) * mask[None]).reshape(256, 256).astype(BF)
        acc[...] += jnp.dot(spread, back[r, :], preferred_element_type=F32)
        return carry

    lax.fori_loop(0, 8, combine, 0)
    out[...] = (resid[...].astype(F32) + (acc[0:128, :] + acc[128:256, :])).astype(BF)

    def drain(j, carry):
        left(rows, dsend, drecv, j)
        left(answers, asend, arecv, j)
        return carry

    lax.fori_loop(0, 8, drain, 0)


def expert_phase(moe_in, resid, place, place_t, chosen, router, w_gate, w_up, w_down):
    vmem = pl.BlockSpec(memory_space=pltpu.VMEM)
    hbm = pl.BlockSpec(memory_space=pl.ANY)
    dma = pltpu.SemaphoreType.DMA
    slots = pltpu.VMEM((2048, 2048), BF)
    return pl.pallas_call(
        experts_kernel,
        name="experts",
        out_shape=jax.ShapeDtypeStruct((128, 2048), BF),
        in_specs=[vmem] * 6 + [hbm] * 3,
        out_specs=vmem,
        scratch_shapes=[
            slots, slots, slots, slots,
            pltpu.VMEM((2048, 768), BF),
            pltpu.VMEM((2048, 768), BF),
            pltpu.VMEM((768, 2048), BF),
            pltpu.VMEM((256, 2048), F32),
            dma((3,)), dma((8,)), dma((8,)), dma((8,)), dma((8,)),
        ],
        compiler_params=pltpu.CompilerParams(
            collective_id=1, has_side_effects=True, vmem_limit_bytes=60 * 1024 * 1024
        ),
    )(moe_in, resid, place, place_t, chosen, router, w_gate, w_up, w_down)


def on_device(
    hidden,
    lengths,
    attn_gain,
    q_gain,
    key_norm_gain,
    w_query,
    key_value_weight,
    w_out,
    ffn_gain,
    w_router,
    routes,
    w_gate,
    w_up,
    w_down,
    page_table,
):
    column = lax.axis_index("exp")
    tokens_here = hidden.shape[0]
    model_width = hidden.shape[1]
    normed = rms_norm(hidden, attn_gain).astype(jnp.bfloat16)
    ends = jnp.cumsum(lengths[0])
    starts = ends - lengths[0]
    lane = jnp.arange(4, dtype=jnp.int32)[:, None]
    index = (lane * 4 + column % 4) * 128 + jnp.arange(128, dtype=jnp.int32)[None, :]
    inside = (index[..., None] >= starts) & (index[..., None] < ends)
    begin = jnp.sum(jnp.where(inside, starts, 0), -1)
    position = (index - begin).astype(jnp.float32)
    freqs = THETA_BASE ** (-jnp.arange(64, dtype=jnp.float32) * 2.0 / 128)
    angles = position[..., None] * freqs
    cosine, sine = jnp.cos(angles), jnp.sin(angles)
    cosf = jnp.concatenate([cosine, cosine], -1)
    sinf = jnp.concatenate([-sine, sine], -1)
    scale = math.log2(math.e) / math.sqrt(128)
    resid, moe_in, own_rows = attention_phase(
        normed, hidden, w_query, key_value_weight, w_out,
        (q_gain * scale).reshape(1, 128), key_norm_gain.reshape(1, 128),
        ffn_gain.reshape(1, 2048), cosf, sinf, begin[..., None],
    )
    expert_count = w_router.shape[1]
    top_count = routes.shape[1]
    capacity = 2 * tokens_here * top_count // expert_count
    req = lax.axis_index("req")
    oy, oc, oz, ox = offset_parts(jnp.arange(expert_count, dtype=jnp.int32))
    to_req = (req // 2 + oy) % 4 * 2 + (req % 2 + oc) % 2
    experts = to_req * 16 + (column // 4 + oz) % 4 * 4 + (column % 4 + ox) % 4
    chosen = jnp.any(routes[:, None, :] == experts[None, :, None], -1)
    token = jnp.arange(tokens_here, dtype=jnp.int32)
    earlier = (token[:, None] < token[None, :]).astype(BF)
    chosen_t = chosen.T
    ranks = jnp.dot(chosen_t.astype(BF), earlier, preferred_element_type=F32).astype(jnp.int32)
    slot = jnp.arange(capacity, dtype=jnp.int32)
    placed = chosen_t[:, None, :] & (ranks[:, None, :] == slot[None, :, None])
    place = placed.astype(BF).reshape(expert_count * capacity, tokens_here)
    order = (experts[None, :] == jnp.arange(expert_count, dtype=jnp.int32)[:, None]).astype(BF)
    router = jnp.dot(w_router, order, preferred_element_type=F32).astype(BF)
    layer_out = expert_phase(
        moe_in, resid, place, place.T, chosen.astype(F32), router, w_gate, w_up, w_down
    )
    blocks_here = page_table.shape[0]
    page_size = tokens_here // blocks_here
    page_width = page_size * own_rows.shape[1]
    page_blocks = own_rows.reshape(blocks_here, page_width)
    req_count = lax.axis_size("req")
    per_peer = blocks_here // req_count
    owner = page_table // blocks_here // lax.axis_size("exp")
    owner_hit = (owner[:, None] == jnp.arange(req_count, dtype=jnp.int32)[None, :]).astype(
        jnp.int32
    )
    rank_inside = jnp.sum((jnp.cumsum(owner_hit, 0) - 1) * owner_hit, 1)
    send_order = owner * per_peer + rank_inside
    send_pages = jnp.zeros_like(page_blocks).at[send_order].set(page_blocks)
    send_slots = jnp.zeros_like(page_table).at[send_order].set(page_table % blocks_here)
    got_pages, got_slots = (
        lax.all_to_all(
            send_pages.reshape(req_count, per_peer, page_width),
            "req",
            split_axis=0,
            concat_axis=0,
            tiled=True,
        ),
        lax.all_to_all(
            send_slots.reshape(req_count, per_peer), "req", split_axis=0, concat_axis=0, tiled=True
        ),
    )
    kv_cache = (
        jnp.zeros_like(page_blocks)
        .at[got_slots.reshape(-1)]
        .set(got_pages.reshape(blocks_here, page_width))
    )
    return (layer_out, kv_cache)


def solution(mesh):
    in_specs = (
        P(("req", "exp"), None),
        P("req", None),
        P(),
        P(),
        P(),
        P(None, "exp"),
        P(),
        P("exp", None),
        P(),
        P(),
        P(("req", "exp"), None),
        P(("req", "exp"), None, None),
        P(("req", "exp"), None, None),
        P(("req", "exp"), None, None),
        P(("req", "exp")),
    )
    out_specs = (P(("req", "exp"), None), P(("req", "exp"), None))
    return jax.shard_map(
        on_device, mesh=mesh, in_specs=in_specs, out_specs=out_specs, check_vma=False
    )
```

```python
import functools
import math

import jax
import jax.numpy as jnp
from jax import lax
from jax.experimental import pallas as pl
from jax.experimental.pallas import tpu as pltpu
from jax.sharding import PartitionSpec as P

EPSILON = 1e-06
THETA_BASE = 1000000.0
MESH = pl.DeviceIdType.MESH
BF = jnp.bfloat16
F32 = jnp.float32


def rms_norm(values, scale_gain):
    values = values.astype(jnp.float32)
    factor = lax.rsqrt(jnp.mean(values * values, -1, keepdims=True) + EPSILON)
    return values * factor * scale_gain


def head_norm_rope(raw, gain, cosf, sinf):
    factor = lax.rsqrt(jnp.mean(raw * raw, -1, keepdims=True) + EPSILON)
    y = raw * factor * gain
    return y * cosf + pltpu.roll(y, 64, 1) * sinf


def attention_kernel(
    normed, hidden, wq, kvw, wo, q_gain, k_gain, ffn_gain, cosf, sinf, start,
    resid_o, moe_o, rows_o,
    tok, wqa, kvv, woa, ka, va, qs, ss, peak, acc, mixed, rs, part,
    lsem, tsend, trecv, wsend, wrecv, osend, orecv, ksend, krecv, rsend, rrecv,
):
    req = lax.axis_index("req")
    col = lax.axis_index("exp")
    z = col // 4
    x = col % 4
    core = req % 2

    def dz(d):
        return (req, lax.rem(z + d, 4) * 4 + x)

    def dx(d):
        return (req, z * 4 + lax.rem(x + d, 4))

    partner = (req + 1 - 2 * core, col)
    z1, z2, z3 = lax.rem(z + 1, 4), lax.rem(z + 2, 4), lax.rem(z + 3, 4)
    x1, x2, x3 = lax.rem(x + 1, 4), lax.rem(x + 2, 4), lax.rem(x + 3, 4)
    sent = []

    def orow(xx, off, size):
        return pl.ds(pl.multiple_of(xx * 256 + off, 64), size)

    def send(src, dst, ssem, rsem, dev):
        c = pltpu.make_async_remote_copy(
            src_ref=src, dst_ref=dst, send_sem=ssem, recv_sem=rsem,
            device_id=dev, device_id_type=MESH,
        )
        c.start()
        sent.append(c)

    def got(dst, rsem, ssem):
        pltpu.make_async_remote_copy(
            src_ref=dst, dst_ref=dst, send_sem=ssem, recv_sem=rsem,
            device_id=partner, device_id_type=MESH,
        ).wait_recv()

    local_kv = pltpu.make_async_copy(kvw, kvv, lsem.at[0])
    local_kv.start()
    local_wq = pltpu.make_async_copy(wq, wqa.at[x], lsem.at[1])
    local_wq.start()
    local_wo = pltpu.make_async_copy(wo, woa.at[orow(x, 0, 256)], lsem.at[2])
    local_wo.start()
    tok[z] = normed[...]
    va[:, 128:256] = jnp.ones((2048, 128), BF)

    barrier = pltpu.get_barrier_semaphore()
    for dev in (dz(1), dz(2), dz(3), dx(1), dx(3), partner):
        pl.semaphore_signal(barrier, inc=1, device_id=dev, device_id_type=MESH)
    pl.semaphore_wait(barrier, 6)

    send(normed, tok.at[z], tsend.at[0], trecv.at[0], dz(1))
    send(normed, tok.at[z], tsend.at[1], trecv.at[1], dz(3))
    half = core * 1024
    send(wq.at[pl.ds(half, 1024)], wqa.at[x, pl.ds(half, 1024)], wsend.at[0], wrecv.at[0], dx(1))
    send(wq.at[pl.ds(half, 1024)], wqa.at[x, pl.ds(half, 1024)], wsend.at[1], wrecv.at[1], dx(3))

    def krow(zz, xx):
        return pl.ds(pl.multiple_of((zz * 4 + xx) * 128, 128), 128)

    def send_kv(zz, j):
        rows = krow(zz, x)
        k = ka.at[rows]
        v = va.at[rows, pl.ds(0, 128)]
        send(k, k, ksend.at[j, 0], krecv.at[j, 0], dx(1))
        send(v, v, ksend.at[j, 1], krecv.at[j, 1], dx(1))
        send(k, k, ksend.at[j, 2], krecv.at[j, 2], dx(3))
        send(v, v, ksend.at[j, 3], krecv.at[j, 3], dx(3))

    def relay_kv(zz, j):
        left = krow(zz, x3)
        right = krow(zz, x1)
        k = ka.at[left]
        got(k, krecv.at[j, 0], ksend.at[j, 0])
        send(k, k, ksend.at[j, 4], krecv.at[j, 4], dx(1))
        v = va.at[right, pl.ds(0, 128)]
        got(v, krecv.at[j, 3], ksend.at[j, 3])
        send(v, v, ksend.at[j, 5], krecv.at[j, 5], dx(3))

    def finish_kv(zz, j):
        left = krow(zz, x3)
        right = krow(zz, x1)
        far = krow(zz, x2)
        got(va.at[left, pl.ds(0, 128)], krecv.at[j, 1], ksend.at[j, 1])
        got(ka.at[right], krecv.at[j, 2], ksend.at[j, 2])
        got(ka.at[far], krecv.at[j, 4], ksend.at[j, 4])
        got(va.at[far, pl.ds(0, 128)], krecv.at[j, 5], ksend.at[j, 5])

    local_kv.wait()
    own = jnp.dot(normed[...], kvv[...], preferred_element_type=F32)
    for h in range(4):
        rows_o[:, h * 128 : (h + 1) * 128] = head_norm_rope(
            own[:, h * 128 : (h + 1) * 128], k_gain[...], cosf[z], sinf[z]
        ).astype(BF)
    rows_o[:, 512:1024] = own[:, 512:1024].astype(BF)
    kcols = pl.ds(pl.multiple_of(z * 128, 128), 128)
    vcols = pl.ds(pl.multiple_of(512 + z * 128, 128), 128)
    ka[krow(z, x), :] = rows_o[:, kcols]
    va[krow(z, x), 0:128] = rows_o[:, vcols]
    send_kv(z, 0)

    def make_kv(zz):
        block = tok[zz]
        kk = jnp.dot(block, kvv[:, kcols], preferred_element_type=F32)
        vv = jnp.dot(block, kvv[:, vcols], preferred_element_type=F32)
        ka[krow(zz, x), :] = head_norm_rope(kk, k_gain[...], cosf[zz], sinf[zz]).astype(BF)
        va[krow(zz, x), 0:128] = vv.astype(BF)

    got(tok.at[z3], trecv.at[0], tsend.at[0])
    send(tok.at[z3, pl.ds(0, 64)], tok.at[z3, pl.ds(0, 64)], tsend.at[2], trecv.at[2], dz(1))
    got(tok.at[z1], trecv.at[1], tsend.at[1])
    send(tok.at[z1, pl.ds(64, 64)], tok.at[z1, pl.ds(64, 64)], tsend.at[3], trecv.at[3], dz(3))
    mine = pl.ds(half, 1024)
    got(wqa.at[x3, mine], wrecv.at[0], wsend.at[0])
    r0 = wqa.at[x3, pl.ds(half, 512)]
    send(r0, r0, wsend.at[2], wrecv.at[2], dx(1))
    got(wqa.at[x1, mine], wrecv.at[1], wsend.at[1])
    r1 = wqa.at[x1, pl.ds(half + 512, 512)]
    send(r1, r1, wsend.at[3], wrecv.at[3], dx(3))
    p0 = wqa.at[x3, mine]
    send(p0, p0, wsend.at[4], wrecv.at[4], partner)
    p1 = wqa.at[x1, mine]
    send(p1, p1, wsend.at[5], wrecv.at[5], partner)

    make_kv(z3)
    send_kv(z3, 1)
    make_kv(z1)
    send_kv(z1, 2)
    relay_kv(z, 0)
    ohalf = core * 128
    omine = pl.ds(ohalf, 128)
    send(wo.at[omine], woa.at[orow(x, ohalf, 128)], osend.at[0], orecv.at[0], dx(1))
    send(wo.at[omine], woa.at[orow(x, ohalf, 128)], osend.at[1], orecv.at[1], dx(3))
    got(tok.at[z2, pl.ds(0, 64)], trecv.at[2], tsend.at[2])
    got(tok.at[z2, pl.ds(64, 64)], trecv.at[3], tsend.at[3])
    make_kv(z2)
    send_kv(z2, 3)
    relay_kv(z3, 1)
    relay_kv(z1, 2)

    got(wqa.at[x2, pl.ds(half, 512)], wrecv.at[2], wsend.at[2])
    got(wqa.at[x2, pl.ds(half + 512, 512)], wrecv.at[3], wsend.at[3])
    p2 = wqa.at[x2, mine]
    send(p2, p2, wsend.at[6], wrecv.at[6], partner)
    local_wq.wait()

    def q_slice(xx):
        for zz in range(2):
            block = jnp.concatenate([tok[2 * zz], tok[2 * zz + 1]], 0)
            raw = jnp.dot(block, wqa[xx], preferred_element_type=F32)
            for b in range(2):
                for h in range(2):
                    y = head_norm_rope(
                        raw[b * 128 : (b + 1) * 128, h * 128 : (h + 1) * 128],
                        q_gain[...], cosf[2 * zz + b], sinf[2 * zz + b],
                    )
                    row = pl.ds(pl.multiple_of((xx * 2 + h) * 128, 128), 128)
                    qs[2 * zz + b, row, :] = y.astype(BF)

    q_slice(x)
    other = pl.ds(1024 - half, 1024)
    got(wqa.at[x3, other], wrecv.at[4], wsend.at[4])
    q_slice(x3)
    relay_kv(z2, 3)
    got(wqa.at[x1, other], wrecv.at[5], wsend.at[5])
    q_slice(x1)
    got(wqa.at[x2, other], wrecv.at[6], wsend.at[6])
    q_slice(x2)

    left_o = woa.at[orow(x3, ohalf, 128)]
    right_o = woa.at[orow(x1, ohalf, 128)]
    far_o = woa.at[orow(x2, ohalf, 128)]
    got(left_o, orecv.at[0], osend.at[0])
    o0 = woa.at[orow(x3, ohalf, 64)]
    send(o0, o0, osend.at[2], orecv.at[2], dx(1))
    got(right_o, orecv.at[1], osend.at[1])
    o1 = woa.at[orow(x1, ohalf + 64, 64)]
    send(o1, o1, osend.at[3], orecv.at[3], dx(3))
    send(left_o, left_o, osend.at[4], orecv.at[4], partner)
    send(right_o, right_o, osend.at[5], orecv.at[5], partner)
    for zz, j in ((z, 0), (z3, 1), (z1, 2), (z2, 3)):
        finish_kv(zz, j)
    last_o = pltpu.make_async_remote_copy(
        src_ref=far_o, dst_ref=far_o, send_sem=osend.at[6], recv_sem=orecv.at[6],
        device_id=partner, device_id_type=MESH,
    )

    def attend(b):
        low = start[b]
        here = (b * 4 + x) * 128 + lax.broadcasted_iota(jnp.int32, (128, 512), 0)
        peak[...] = jnp.full((1024, 128), -1e30, F32)

        def score_step(c, carry):
            keys = pl.ds(pl.multiple_of(c * 512, 512), 512)
            s = lax.dot_general(
                qs[b], ka[keys, :], (((1,), (1,)), ((), ())), preferred_element_type=F32
            )
            kid = c * 512 + lax.broadcasted_iota(jnp.int32, (128, 512), 1)
            bias = jnp.where((kid >= low) & (kid <= here), 0.0, -1e30)
            s = (s.reshape(8, 128, 512) + bias[None]).reshape(1024, 512)
            ss[:, keys] = s
            top = peak[...]
            for g in range(4):
                top = jnp.maximum(top, s[:, g * 128 : (g + 1) * 128])
            peak[...] = top
            return carry

        lax.fori_loop(0, b + 1, score_step, 0)
        peak[...] = jnp.broadcast_to(jnp.max(peak[...], -1, keepdims=True), (1024, 128))
        acc[...] = jnp.zeros((1024, 256), F32)

        def mix_step(c, carry):
            keys = pl.ds(pl.multiple_of(c * 512, 512), 512)
            p = jnp.exp2(ss[:, keys] - peak[:, 0:1]).astype(BF)
            acc[...] += jnp.dot(p, va[keys, :], preferred_element_type=F32)
            return carry

        lax.fori_loop(0, b + 1, mix_step, 0)
        for h in range(8):
            rows = slice(h * 128, (h + 1) * 128)
            mixed[:, h * 128 : (h + 1) * 128] = (acc[rows, 0:128] / acc[rows, 128:256]).astype(BF)

    def share(i, off):
        b = lax.rem(z + off, 4)
        return pltpu.make_async_remote_copy(
            src_ref=part.at[b], dst_ref=rs.at[z], send_sem=rsend.at[i], recv_sem=rrecv.at[i],
            device_id=(req, b * 4 + x), device_id_type=MESH,
        )

    def block_step(i, carry):
        off = jnp.where(i == 0, 2, jnp.where(i == 1, 1, jnp.where(i == 2, 3, 0)))
        b = lax.rem(z + off, 4)
        attend(b)

        @pl.when(i == 0)
        def _():
            got(woa.at[orow(x2, ohalf, 64)], orecv.at[2], osend.at[2])
            got(woa.at[orow(x2, ohalf + 64, 64)], orecv.at[3], osend.at[3])
            last_o.start()
            got(woa.at[orow(x3, 128 - ohalf, 128)], orecv.at[4], osend.at[4])
            got(woa.at[orow(x1, 128 - ohalf, 128)], orecv.at[5], osend.at[5])
            got(woa.at[orow(x2, 128 - ohalf, 128)], orecv.at[6], osend.at[6])
            local_wo.wait()

        for n in range(2):
            cols = slice(n * 1024, (n + 1) * 1024)
            part[b, :, cols] = jnp.dot(
                mixed[...], woa[:, cols], preferred_element_type=F32
            ).astype(BF)

        @pl.when(i < 3)
        def _():
            share(i, off).start()

        return carry

    lax.fori_loop(0, 4, block_step, 0)
    for i, off in enumerate((2, 1, 3)):
        src = lax.rem(z + 4 - off, 4)
        got(rs.at[src], rrecv.at[i], rsend.at[i])
    total = hidden[...].astype(F32) + part[z].astype(F32)
    for d in range(1, 4):
        total = total + rs[lax.rem(z + d, 4)].astype(F32)
    resid = total.astype(BF)
    resid_o[...] = resid
    rf = resid.astype(F32)
    factor = lax.rsqrt(jnp.mean(rf * rf, -1, keepdims=True) + EPSILON)
    moe_o[...] = (rf * factor * ffn_gain[...]).astype(BF)
    for c in sent:
        c.wait_send()
    last_o.wait_send()
    for i, off in enumerate((2, 1, 3)):
        share(i, off).wait_send()


def attention_phase(normed, hidden, w_query, key_value_weight, w_out, q_gain, k_gain, ffn_gain, cosf, sinf, start):
    vmem = pl.BlockSpec(memory_space=pltpu.VMEM)
    hbm = pl.BlockSpec(memory_space=pl.ANY)
    dma = pltpu.SemaphoreType.DMA
    return pl.pallas_call(
        attention_kernel,
        name="attention",
        out_shape=(
            jax.ShapeDtypeStruct((128, 2048), BF),
            jax.ShapeDtypeStruct((128, 2048), BF),
            jax.ShapeDtypeStruct((128, 1024), BF),
        ),
        in_specs=[vmem, vmem, hbm, hbm, hbm, vmem, vmem, vmem, vmem, vmem, vmem],
        out_specs=(vmem, vmem, vmem),
        scratch_shapes=[
            pltpu.VMEM((4, 128, 2048), BF),
            pltpu.VMEM((4, 2048, 256), BF),
            pltpu.VMEM((2048, 1024), BF),
            pltpu.VMEM((1024, 2048), BF),
            pltpu.VMEM((2048, 128), BF),
            pltpu.VMEM((2048, 256), BF),
            pltpu.VMEM((4, 1024, 128), BF),
            pltpu.VMEM((1024, 2048), F32),
            pltpu.VMEM((1024, 128), F32),
            pltpu.VMEM((1024, 256), F32),
            pltpu.VMEM((128, 1024), BF),
            pltpu.VMEM((4, 128, 2048), BF),
            pltpu.VMEM((4, 128, 2048), BF),
            dma((3,)), dma((4,)), dma((4,)), dma((7,)), dma((7,)), dma((7,)), dma((7,)),
            dma((4, 6)), dma((4, 6)), dma((3,)), dma((3,)),
        ],
        compiler_params=pltpu.CompilerParams(
            collective_id=0, has_side_effects=True, vmem_limit_bytes=60 * 1024 * 1024
        ),
    )(normed, hidden, w_query, key_value_weight, w_out, q_gain, k_gain, ffn_gain, cosf, sinf, start)


def offset_parts(i):
    chunk = lax.div(i, 16)
    inner = lax.rem(i, 16)
    oy, oz = lax.div(inner, 4), lax.rem(inner, 4)
    ox = lax.rem(lax.rem(chunk, 4) + 8 - oy - oz, 4)
    return oy, lax.div(chunk, 4), oz, ox


def experts_kernel(
    moe, resid, place, place_t, chosen, router, own, turn, goal, wg, wu, wd,
    out, cache,
    rows, batch, answers, back, wgv, wuv, wdv, acc,
    pages, got_pages, got_goal,
    lsem, dsend, drecv, asend, arecv, psend, precv, gsend, grecv,
):
    req = lax.axis_index("req")
    col = lax.axis_index("exp")
    y, core = lax.div(req, 2), lax.rem(req, 2)
    z, x = lax.div(col, 4), lax.rem(col, 4)

    def target(i):
        oy, oc, oz, ox = offset_parts(i)
        return (
            lax.rem(y + oy, 4) * 2 + core + oc - 2 * core * oc,
            lax.rem(z + oz, 4) * 4 + lax.rem(x + ox, 4),
        )

    def origin(i):
        oy, oc, oz, ox = offset_parts(i)
        return (
            lax.rem(y + 4 - oy, 4) * 2 + core + oc - 2 * core * oc,
            lax.rem(z + 4 - oz, 4) * 4 + lax.rem(x + 4 - ox, 4),
        )

    loads = [
        pltpu.make_async_copy(src.at[0], dst, lsem.at[n])
        for n, (src, dst) in enumerate(((wg, wgv), (wu, wuv), (wd, wdv)))
    ]
    for c in loads:
        c.start()

    barrier = pltpu.get_barrier_semaphore()

    def greet(i, carry):
        pl.semaphore_signal(barrier, inc=1, device_id=target(i), device_id_type=MESH)
        return carry

    lax.fori_loop(1, 128, greet, 0)

    def chunk_rows(j):
        return pl.ds(pl.multiple_of(j * 256, 256), 256)

    def build(j, carry):
        r = chunk_rows(j)
        rows[r, :] = jnp.dot(place[r, :], moe[...], preferred_element_type=F32).astype(BF)
        return carry

    lax.fori_loop(0, 8, build, 0)
    batch[0:16, :] = rows[0:16, :]

    pages[...] = jnp.dot(turn[...], own[...], preferred_element_type=F32).astype(BF)

    def page(r):
        return pl.ds(pl.multiple_of(r * 16, 16), 16)

    got_pages[page(req), :] = pages[page(req), :]
    got_goal[page(req), :] = goal[page(req), :]
    pl.semaphore_wait(barrier, 127)

    def page_copies(d, there, here):
        dev = (lax.rem(req + d, 8), col)
        return [
            pltpu.make_async_remote_copy(
                src_ref=src.at[page(there)], dst_ref=dst.at[page(here)],
                send_sem=ssem.at[d], recv_sem=rsem.at[d], device_id=dev, device_id_type=MESH,
            )
            for src, dst, ssem, rsem in (
                (pages, got_pages, psend, precv), (goal, got_goal, gsend, grecv)
            )
        ]

    for d in range(1, 8):
        for c in page_copies(d, lax.rem(req + d, 8), req):
            c.start()

    def dispatch(i, carry):
        r = pl.ds(pl.multiple_of(i * 16, 16), 16)
        pltpu.make_async_remote_copy(
            src_ref=rows.at[r], dst_ref=batch.at[r],
            send_sem=dsend.at[lax.div(i, 16)], recv_sem=drecv.at[lax.div(i, 16)],
            device_id=target(i), device_id_type=MESH,
        ).start()
        return carry

    lax.fori_loop(1, 128, dispatch, 0)

    def whole(buf, ssem, rsem, j, r):
        return pltpu.make_async_remote_copy(
            src_ref=buf.at[r], dst_ref=buf.at[r], send_sem=ssem.at[j], recv_sem=rsem.at[j],
            device_id=target(1), device_id_type=MESH,
        )

    def arrived(buf, ssem, rsem, j):
        @pl.when(j == 0)
        def _():
            whole(buf, ssem, rsem, j, pl.ds(16, 240)).wait_recv()

        @pl.when(j > 0)
        def _():
            whole(buf, ssem, rsem, j, chunk_rows(j)).wait_recv()

    def left(buf, ssem, rsem, j):
        @pl.when(j == 0)
        def _():
            whole(buf, ssem, rsem, j, pl.ds(16, 240)).wait_send()

        @pl.when(j > 0)
        def _():
            whole(buf, ssem, rsem, j, chunk_rows(j)).wait_send()

    logits = jnp.dot(moe[...], router[...], preferred_element_type=F32)
    grown = jnp.exp(logits - jnp.max(logits, -1, keepdims=True))
    soft = grown / jnp.sum(grown, -1, keepdims=True)
    picked = soft * chosen[...]
    gates = picked / jnp.sum(picked, -1, keepdims=True)
    high = gates.astype(BF)
    low = (gates - high.astype(F32)).astype(BF)
    both = jnp.concatenate([high, low], 0)
    acc[...] = jnp.zeros((256, 2048), F32)
    for c in loads:
        c.wait()

    def work(j, carry):
        arrived(batch, dsend, drecv, j)
        r = chunk_rows(j)
        taken = batch[r, :]
        g = jnp.dot(taken, wgv[...], preferred_element_type=F32)
        u = jnp.dot(taken, wuv[...], preferred_element_type=F32)
        act = (g / (1.0 + jnp.exp(-g)) * u).astype(BF)
        answers[r, :] = jnp.dot(act, wdv[...], preferred_element_type=F32).astype(BF)

        def reply(q, inner):
            i = j * 16 + q
            p = pl.ds(pl.multiple_of(i * 16, 16), 16)
            pltpu.make_async_remote_copy(
                src_ref=answers.at[p], dst_ref=back.at[p],
                send_sem=asend.at[j], recv_sem=arecv.at[j],
                device_id=origin(i), device_id_type=MESH,
            ).start()
            return inner

        @pl.when(j == 0)
        def _():
            back[0:16, :] = answers[0:16, :]
            lax.fori_loop(1, 16, reply, 0)

        @pl.when(j > 0)
        def _():
            lax.fori_loop(0, 16, reply, 0)

        return carry

    lax.fori_loop(0, 8, work, 0)

    for d in range(1, 8):
        for c in page_copies(d, lax.rem(req + d, 8), lax.rem(req + 8 - d, 8)):
            c.wait_recv()
    at = lax.broadcasted_iota(jnp.int32, (128, 128), 1)
    settle = jnp.where(got_goal[...] == at, 1.0, 0.0).T.astype(BF)
    cache[...] = jnp.dot(settle, got_pages[...], preferred_element_type=F32).astype(BF)

    def combine(j, carry):
        arrived(back, asend, arecv, j)
        r = chunk_rows(j)
        expert = lax.broadcasted_iota(jnp.int32, (128, 256), 0)
        owner = j * 16 + lax.broadcasted_iota(jnp.int32, (128, 256), 1) // 16
        pick = jnp.where(expert == owner, 1.0, 0.0).astype(BF)
        spread = jnp.dot(both, pick, preferred_element_type=F32)
        mask = place_t[:, r].astype(F32)
        spread = (spread.reshape(2, 128, 256) * mask[None]).reshape(256, 256).astype(BF)
        acc[...] += jnp.dot(spread, back[r, :], preferred_element_type=F32)
        return carry

    lax.fori_loop(0, 8, combine, 0)
    out[...] = (resid[...].astype(F32) + (acc[0:128, :] + acc[128:256, :])).astype(BF)

    def drain(j, carry):
        left(rows, dsend, drecv, j)
        left(answers, asend, arecv, j)
        return carry

    lax.fori_loop(0, 8, drain, 0)
    for d in range(1, 8):
        for c in page_copies(d, lax.rem(req + d, 8), req):
            c.wait_send()


def expert_phase(moe_in, resid, place, place_t, chosen, router, own, turn, goal, w_gate, w_up, w_down):
    vmem = pl.BlockSpec(memory_space=pltpu.VMEM)
    hbm = pl.BlockSpec(memory_space=pl.ANY)
    dma = pltpu.SemaphoreType.DMA
    slots = pltpu.VMEM((2048, 2048), BF)
    return pl.pallas_call(
        experts_kernel,
        name="experts",
        out_shape=(
            jax.ShapeDtypeStruct((128, 2048), BF),
            jax.ShapeDtypeStruct((128, 1024), BF),
        ),
        in_specs=[vmem] * 9 + [hbm] * 3,
        out_specs=(vmem, vmem),
        scratch_shapes=[
            slots, slots, slots, slots,
            pltpu.VMEM((2048, 768), BF),
            pltpu.VMEM((2048, 768), BF),
            pltpu.VMEM((768, 2048), BF),
            pltpu.VMEM((256, 2048), F32),
            pltpu.VMEM((128, 1024), BF),
            pltpu.VMEM((128, 1024), BF),
            pltpu.VMEM((128, 128), jnp.int32),
            dma((3,)), dma((8,)), dma((8,)), dma((8,)), dma((8,)),
            dma((8,)), dma((8,)), dma((8,)), dma((8,)),
        ],
        compiler_params=pltpu.CompilerParams(
            collective_id=1, has_side_effects=True, vmem_limit_bytes=60 * 1024 * 1024
        ),
    )(moe_in, resid, place, place_t, chosen, router, own, turn, goal, w_gate, w_up, w_down)


def on_device(
    hidden,
    lengths,
    attn_gain,
    q_gain,
    key_norm_gain,
    w_query,
    key_value_weight,
    w_out,
    ffn_gain,
    w_router,
    routes,
    w_gate,
    w_up,
    w_down,
    page_table,
):
    column = lax.axis_index("exp")
    tokens_here = hidden.shape[0]
    model_width = hidden.shape[1]
    normed = rms_norm(hidden, attn_gain).astype(jnp.bfloat16)
    ends = jnp.cumsum(lengths[0])
    starts = ends - lengths[0]
    lane = jnp.arange(4, dtype=jnp.int32)[:, None]
    index = (lane * 4 + column % 4) * 128 + jnp.arange(128, dtype=jnp.int32)[None, :]
    inside = (index[..., None] >= starts) & (index[..., None] < ends)
    begin = jnp.sum(jnp.where(inside, starts, 0), -1)
    position = (index - begin).astype(jnp.float32)
    freqs = THETA_BASE ** (-jnp.arange(64, dtype=jnp.float32) * 2.0 / 128)
    angles = position[..., None] * freqs
    cosine, sine = jnp.cos(angles), jnp.sin(angles)
    cosf = jnp.concatenate([cosine, cosine], -1)
    sinf = jnp.concatenate([-sine, sine], -1)
    scale = math.log2(math.e) / math.sqrt(128)
    resid, moe_in, own_rows = attention_phase(
        normed, hidden, w_query, key_value_weight, w_out,
        (q_gain * scale).reshape(1, 128), key_norm_gain.reshape(1, 128),
        ffn_gain.reshape(1, 2048), cosf, sinf, begin[..., None],
    )
    expert_count = w_router.shape[1]
    top_count = routes.shape[1]
    capacity = 2 * tokens_here * top_count // expert_count
    req = lax.axis_index("req")
    oy, oc, oz, ox = offset_parts(jnp.arange(expert_count, dtype=jnp.int32))
    to_req = (req // 2 + oy) % 4 * 2 + (req % 2 + oc) % 2
    experts = to_req * 16 + (column // 4 + oz) % 4 * 4 + (column % 4 + ox) % 4
    chosen = jnp.any(routes[:, None, :] == experts[None, :, None], -1)
    token = jnp.arange(tokens_here, dtype=jnp.int32)
    earlier = (token[:, None] < token[None, :]).astype(BF)
    chosen_t = chosen.T
    ranks = jnp.dot(chosen_t.astype(BF), earlier, preferred_element_type=F32).astype(jnp.int32)
    slot = jnp.arange(capacity, dtype=jnp.int32)
    placed = chosen_t[:, None, :] & (ranks[:, None, :] == slot[None, :, None])
    place = placed.astype(BF).reshape(expert_count * capacity, tokens_here)
    order = (experts[None, :] == jnp.arange(expert_count, dtype=jnp.int32)[:, None]).astype(BF)
    router = jnp.dot(w_router, order, preferred_element_type=F32).astype(BF)
    blocks_here = page_table.shape[0]
    page_size = tokens_here // blocks_here
    owner = page_table // blocks_here // lax.axis_size("exp")
    peer, inside_page = token // page_size, token % page_size
    from_block = owner[None, :] == jnp.arange(blocks_here, dtype=jnp.int32)[:, None]
    spot = jnp.sum(jnp.where(from_block, page_table % blocks_here, 0), 1)
    same = inside_page[:, None] == inside_page[None, :]
    turn = (jnp.repeat(owner, page_size)[None, :] == peer[:, None]) & same
    goal = jnp.repeat(spot, page_size) * page_size + inside_page
    layer_out, cache_rows = expert_phase(
        moe_in, resid, place, place.T, chosen.astype(F32), router, own_rows, turn.astype(BF),
        jnp.broadcast_to(goal[:, None], (tokens_here, 128)), w_gate, w_up, w_down,
    )
    kv_cache = cache_rows.reshape(blocks_here, page_size * own_rows.shape[1])
    return (layer_out, kv_cache)


def solution(mesh):
    in_specs = (
        P(("req", "exp"), None),
        P("req", None),
        P(),
        P(),
        P(),
        P(None, "exp"),
        P(),
        P("exp", None),
        P(),
        P(),
        P(("req", "exp"), None),
        P(("req", "exp"), None, None),
        P(("req", "exp"), None, None),
        P(("req", "exp"), None, None),
        P(("req", "exp")),
    )
    out_specs = (P(("req", "exp"), None), P(("req", "exp"), None))
    return jax.shard_map(
        on_device, mesh=mesh, in_specs=in_specs, out_specs=out_specs, check_vma=False
    )
```
